256 devices in a mesh: row: 16 (over z, core), col: 16 (over x, y).
Axes of the slice: x: 4, y: 4, z: 8, core: 2. Of those that a mesh axis runs over, the one named last changes fastest.
Arguments:
- source_emb: bfloat16 [65536, 256], P(('col', 'row')), may hold values from -6 to 6
- self_feat: bfloat16 [65536, 256], P(('row', 'col')), may hold values from -6 to 6
- w_self: bfloat16 [256, 256], replicated, may hold values from -0.375 to 0.375
- w_neigh: bfloat16 [256, 256], replicated, may hold values from -0.375 to 0.375
- bias: float32 [256], replicated, may hold values from -3 to 3
- cotangent: bfloat16 [65536, 256], P(('row', 'col')), may hold values from -6 to 6
- tile_dst: int32 [16, 16, 128], P('row', 'col'), may hold values from 0 to 31, as said below
- tile_src: int32 [16, 16, 128], P('row', 'col'), may hold values from 0 to 31
- tile_live: int32 [16, 16], P('row', 'col'), may hold values from 1 to 128, as said below
- tile_counts: int32 [16, 16, 128, 128, 128], P('row', 'col'), may hold values from 0 to 3, as said below
Outputs:
- layer_out: bfloat16 [65536, 256], P(('row', 'col'))
- grad_self: bfloat16 [65536, 256], P(('row', 'col'))
- grad_source: bfloat16 [65536, 256], P(('col', 'row'))
- grad_w_self: float32 [256, 256], replicated
- grad_w_neigh: float32 [256, 256], replicated
- grad_bias: float32 [256], replicated
The draws below stay inside these ranges and needn't reach their ends.
Inputs may be any that keep to these rules, and one draw needn't show every extreme that they name: Within one grid cell the pairs (tile_dst, tile_src) of all 128 slots are distinct. `tile_live`: some grid cell uses all 128 slots in every draw. `tile_counts`: slots at or past tile_live hold counts too, which are ignored.
All inputs are finite; a program needn't handle non-finite values.
Results may differ from the reference program's by a relative error of at most 0.007.
Values may be sent and summed in bfloat16 or wider, within the bound.
A program may use at most 128 MiB of HBM per device.

```python
import math
import jax
import jax.numpy as jnp
from jax import lax

H = 256
BLOCK = 128
NDST = 65536
NSRC = 65536
DST_BLOCKS = 32
SRC_BLOCKS = 32
TILES = 128
N_ROW = 16
N_COL = 16


def tile_coords(key):
    base = jax.random.fold_in(key, 11)
    cell_keys = jax.random.split(base, N_ROW * N_COL)

    def one_cell(cell_key):
        return jax.random.permutation(cell_key, DST_BLOCKS * SRC_BLOCKS)[:TILES]
    picked = jax.vmap(one_cell)(cell_keys)
    return picked.reshape(N_ROW, N_COL, TILES).astype(jnp.int32)


def draw_tile_dst(key, part):
    return (tile_coords(key) // SRC_BLOCKS).astype(jnp.int32)


def draw_tile_src(key, part):
    return (tile_coords(key) % SRC_BLOCKS).astype(jnp.int32)


def draw_tile_live(key, part):
    base = jax.random.fold_in(key, 23)
    key_one, key_two, key_three = jax.random.split(base, 3)
    lowest = max(1, TILES // 8)
    first_draw = jax.random.randint(key_one, (N_ROW * N_COL,), lowest, TILES + 1)
    second_draw = jax.random.randint(key_two, (N_ROW * N_COL,), lowest, TILES + 1)
    live_count = jnp.minimum(first_draw, second_draw)
    full_cell = jax.random.randint(key_three, (), 0, N_ROW * N_COL)
    live_count = jnp.where(jnp.arange(N_ROW * N_COL) == full_cell, TILES, live_count)
    return live_count.reshape(N_ROW, N_COL).astype(jnp.int32)


def draw_tile_counts(key, part):
    base = jax.random.fold_in(key, 37)
    raw_values = jax.random.randint(base, (N_ROW, N_COL, TILES, BLOCK, BLOCK), 0, 96)
    cutoff = max(3, 384 // BLOCK)
    return jnp.where(raw_values < cutoff, 1 + raw_values % 3, 0).astype(jnp.int32)


def levels(stream_key, shape, pieces, smallest, top_value):
    level = 1.0
    for position, shards_of in pieces:
        steps = jax.random.uniform(jax.random.fold_in(jax.random.fold_in(stream_key, 6), position), (shards_of,), jnp.float32, smallest / len(pieces), top_value / len(pieces))
        level = level * jnp.repeat(jnp.exp(steps), shape[position] // shards_of).reshape((-1,) + (1,) * (len(shape) - 1 - position))
    return level


def normal_values(stream_key, shape, scale, most, shards=(), kind=jnp.bfloat16):
    drawn = scale * jax.random.normal(stream_key, shape, jnp.float32)
    if shards:
        drawn = drawn * levels(stream_key, shape, shards, -0.22, 0.18)
    return jnp.clip(drawn, -most, most).astype(kind)


def setup_inputs(seed: int = 0) -> dict:
    streams_of = jax.random.split(jax.random.key(seed), 11)
    source_emb = normal_values(streams_of[0], (NSRC, H), 1.0, 6.0, ((0, 256),))
    self_feat = normal_values(streams_of[1], (NDST, H), 1.0, 6.0, ((0, 256),))
    w_self = normal_values(streams_of[2], (H, H), H ** -0.5, 0.375)
    w_neigh = normal_values(streams_of[3], (H, H), H ** -0.5, 0.375)
    bias = normal_values(streams_of[4], (H,), 0.5, 3.0, (), jnp.float32)
    cotangent = normal_values(streams_of[5], (NDST, H), 1.0, 6.0, ((0, 256),))
    tile_dst = draw_tile_dst(jax.random.fold_in(streams_of[10], 71), 0)
    tile_src = draw_tile_src(jax.random.fold_in(streams_of[10], 71), 0)
    tile_live = draw_tile_live(jax.random.fold_in(streams_of[10], 71), 0)
    tile_counts = draw_tile_counts(jax.random.fold_in(streams_of[10], 71), 0)
    return {"source_emb": source_emb, "self_feat": self_feat, "w_self": w_self, "w_neigh": w_neigh, "bias": bias, "cotangent": cotangent, "tile_dst": tile_dst, "tile_src": tile_src, "tile_live": tile_live, "tile_counts": tile_counts}


def reference(source_emb, self_feat, w_self, w_neigh, bias, cotangent, tile_dst, tile_src, tile_live, tile_counts):
    dst_slab = NDST // N_ROW
    src_slab = NSRC // N_COL
    cell_count = N_ROW * N_COL
    row_of = jnp.arange(cell_count, dtype=jnp.int32) // N_COL
    col_of = jnp.arange(cell_count, dtype=jnp.int32) % N_COL
    dst_first = (row_of[:, None] * dst_slab + tile_dst.reshape(cell_count, TILES) * BLOCK).reshape(-1).astype(jnp.int32)
    src_first = (col_of[:, None] * src_slab + tile_src.reshape(cell_count, TILES) * BLOCK).reshape(-1).astype(jnp.int32)
    slot_used = (jnp.arange(TILES, dtype=jnp.int32)[None, :] < tile_live.reshape(cell_count, 1)).reshape(-1)
    all_counts = tile_counts.reshape(cell_count * TILES, BLOCK, BLOCK)

    def forward_step(running, element):
        neighbor_sum, degree = running
        tile_count, used_flag, dst_at, src_at = element
        weights = jnp.where(used_flag, tile_count, 0).astype(jnp.bfloat16)
        block_rows = lax.dynamic_slice_in_dim(source_emb, src_at, BLOCK, 0)
        tile_term = jnp.dot(weights, block_rows, preferred_element_type=jnp.float32)
        current = lax.dynamic_slice_in_dim(neighbor_sum, dst_at, BLOCK, 0)
        neighbor_sum = lax.dynamic_update_slice_in_dim(neighbor_sum, current + tile_term, dst_at, 0)
        deg_now = lax.dynamic_slice_in_dim(degree, dst_at, BLOCK, 0)
        degree = lax.dynamic_update_slice_in_dim(degree, deg_now + lax.optimization_barrier(jnp.sum(weights.astype(jnp.float32), axis=1)), dst_at, 0)
        return ((neighbor_sum, degree), None)
    start_sum = jnp.zeros((NDST, H), jnp.float32)
    start_deg = jnp.zeros((NDST,), jnp.float32)
    (neighbor_sum, degree), _ = lax.scan(forward_step, (start_sum, start_deg), (all_counts, slot_used, dst_first, src_first))
    inv_root = 1.0 / jnp.sqrt(degree + 1.0)
    aggregate = (neighbor_sum * inv_root[:, None]).astype(jnp.bfloat16)
    preact = jnp.dot(self_feat, w_self, preferred_element_type=jnp.float32) + jnp.dot(aggregate, w_neigh, preferred_element_type=jnp.float32) + bias
    layer_out = jax.nn.silu(preact).astype(jnp.bfloat16)
    sigmoid_z = jax.nn.sigmoid(preact)
    grad_pre = (cotangent.astype(jnp.float32) * sigmoid_z * (1.0 + preact * (1.0 - sigmoid_z))).astype(jnp.bfloat16)
    scale = 1.0 / math.sqrt(NDST)
    grad_w_self = jnp.dot(self_feat.T, grad_pre, preferred_element_type=jnp.float32) * scale
    grad_w_neigh = jnp.dot(aggregate.T, grad_pre, preferred_element_type=jnp.float32) * scale
    grad_bias = lax.optimization_barrier(jnp.sum(grad_pre.astype(jnp.float32), axis=0)) * scale
    grad_self = jnp.dot(grad_pre, w_self.T, preferred_element_type=jnp.float32).astype(jnp.bfloat16)
    grad_sum = (jnp.dot(grad_pre, w_neigh.T, preferred_element_type=jnp.float32) * inv_root[:, None]).astype(jnp.bfloat16)

    def backward_step(back_sum, element):
        tile_count, used_flag, dst_at, src_at = element
        weights = jnp.where(used_flag, tile_count, 0).astype(jnp.bfloat16)
        block_rows = lax.dynamic_slice_in_dim(grad_sum, dst_at, BLOCK, 0)
        tile_term = jnp.dot(weights.T, block_rows, preferred_element_type=jnp.float32)
        current = lax.dynamic_slice_in_dim(back_sum, src_at, BLOCK, 0)
        back_sum = lax.dynamic_update_slice_in_dim(back_sum, current + tile_term, src_at, 0)
        return (back_sum, None)
    back_sum, _ = lax.scan(backward_step, jnp.zeros((NSRC, H), jnp.float32), (all_counts, slot_used, dst_first, src_first))
    grad_source = back_sum.astype(jnp.bfloat16)
    return (layer_out, grad_self, grad_source, grad_w_self, grad_w_neigh, grad_bias)
```

```python
import functools
import math

import jax
import jax.numpy as jnp
from jax import lax
from jax.experimental import pallas as pl
from jax.experimental.pallas import tpu as pltpu
from jax.sharding import PartitionSpec as P

F32, BF16 = jnp.float32, jnp.bfloat16
MESH = pl.DeviceIdType.MESH
NZ, NX, NY = 8, 4, 4
NB = 32
SLOTS = 128
ZERO_SLOT = SLOTS


def rcopy(src, dst, ssem, rsem, **where):
    return pltpu.make_async_remote_copy(
        src_ref=src, dst_ref=dst, send_sem=ssem, recv_sem=rsem, device_id=where, device_id_type=MESH
    )


def kernel(
    scale,
    sel, dkey, emb, feat, w_self, w_neigh, bias, cot, counts,
    layer_out, grad_self, grad_source, g_ws, g_wn, g_b,
    stage, cnt, cnt_t, acc, tab, sa, sb, ra, rb, s2a, s2b, r2a, r2b, nsum, rsum, dg0, dg1, dg2, dg3,
    agg, gpre, dtab, ws1, wr1, ws2, wr2, wps, wpr, wz, wg, psend, precv, usend, urecv, dsend, drecv,
    csem, ag_r, ag_su, ag_sd, ag_sp, sa_s, sa_r, sb_s, sb_r, s2a_s, s2a_r, s2b_s, s2b_r,
    dgx_s, dgx_r, dgy_s, dgy_r, df_s, df_r, da_s, da_r, db_s, db_r,
    w1_s, w1_r, w2_s, w2_r, wp_s, wp_r, wz_s, wz_r, wy_s, wy_r, wx_s, wx_r,
    p_s, p_r, u_s, u_r, d_s, d_r,
):
    me_r, me_c = lax.axis_index("row"), lax.axis_index("col")
    z, k = me_r // 2, me_r % 2
    x, y = me_c // NY, me_c % NY
    kp = 1 - k

    def zm(v):
        return (v + 2 * NZ) % NZ

    def rw(zz, kk):
        return zm(zz) * 2 + kk

    def xm(j):
        return (x + j) % NX

    def ym(j):
        return (y + j) % NY

    def cl(xx, yy):
        return xx * NY + yy

    partner = rw(z, kp)

    def count_copy(i):
        part = pl.ds(i * 8, 8)
        return pltpu.make_async_copy(counts.at[part], stage.at[part], csem.at[i])

    def start_counts(i, carry):
        count_copy(i).start()
        return carry

    lax.fori_loop(0, 16, start_counts, 0)

    barrier = pltpu.get_barrier_semaphore()

    def greet_z(j, carry):
        pl.semaphore_signal(barrier, inc=1, device_id={"row": rw(z + j, k)}, device_id_type=MESH)
        return carry

    def greet_xy(j, carry):
        pl.semaphore_signal(barrier, inc=1, device_id={"col": cl(xm(j), y)}, device_id_type=MESH)
        pl.semaphore_signal(barrier, inc=1, device_id={"col": cl(x, ym(j))}, device_id_type=MESH)
        return carry

    pl.semaphore_signal(barrier, inc=1, device_id={"row": partner}, device_id_type=MESH)
    lax.fori_loop(1, NZ, greet_z, 0)
    lax.fori_loop(1, NX, greet_xy, 0)
    pl.semaphore_wait(barrier, 1 + (NZ - 1) + 2 * (NX - 1))

    def ag_up(src, r, u):
        return rcopy(src, tab.at[r], ag_su.at[u], ag_r.at[r], row=rw(z + 1, k))

    def ag_down(src, r, u):
        return rcopy(src, tab.at[r], ag_sd.at[u], ag_r.at[r], row=rw(z - 1, k))

    def ag_partner(src, r):
        return rcopy(src, tab.at[r], ag_sp.at[r // 2], ag_r.at[r], row=partner)

    def ag_wait(r):
        rcopy(tab.at[r], tab.at[r], ag_sp.at[r // 2], ag_r.at[r], row=partner).wait_recv()

    ag_up(emb, me_r, 0).start()
    ag_down(emb, me_r, 0).start()
    ag_partner(emb, me_r).start()
    tab[me_r] = emb[...]
    cnt[ZERO_SLOT] = jnp.zeros((128, 128), BF16)
    cnt_t[ZERO_SLOT] = jnp.zeros((128, 128), BF16)

    def zero_acc(i, carry):
        acc[pl.ds(pl.multiple_of(i * 256, 256), 256), :] = jnp.zeros((256, 256), F32)
        return carry

    lax.fori_loop(0, 16, zero_acc, 0)

    def convert(i, carry):
        count_copy(i).wait()
        part = pl.ds(i * 8, 8)
        cnt[part] = stage[part].astype(F32).astype(BF16)
        return carry

    lax.fori_loop(0, 16, convert, 0)

    def spmm(tiles, table, s0, s1, place):
        def block(b, carry):
            rows = []
            for i in range(8):
                d = b * 8 + i
                rows.append(
                    jnp.concatenate(
                        [
                            tiles[sel[place(d, 2 * s0)]],
                            tiles[sel[place(d, 2 * s0 + 1)]],
                            tiles[sel[place(d, 2 * s1)]],
                            tiles[sel[place(d, 2 * s1 + 1)]],
                        ],
                        axis=1,
                    )
                )
            lhs = jnp.concatenate(rows, axis=0)
            rhs = jnp.concatenate([table[s0], table[s1]], axis=0)
            r = pl.ds(pl.multiple_of(b * 1024, 1024), 1024)
            acc[r, :] += jnp.dot(lhs, rhs, preferred_element_type=F32)
            return carry

        lax.fori_loop(0, NB // 8, block, 0)

    def fwd_place(d, s):
        return d * NB + s

    def bwd_place(s, d):
        return d * NB + s

    def ag_step(t, carry):
        up, down = rw(z - t - 1, k), rw(z + t + 1, k)
        ag_wait(up)

        @pl.when(t < 3)
        def _():
            ag_up(tab.at[up], up, t + 1).start()

        ag_partner(tab.at[up], up).start()

        @pl.when(t < 3)
        def _():
            ag_wait(down)

            @pl.when(t < 2)
            def _():
                ag_down(tab.at[down], down, t + 1).start()

            ag_partner(tab.at[down], down).start()
            ag_wait(rw(z - t, kp))

        @pl.when(t == 3)
        def _():
            ag_wait(rw(z - t, kp))

        @pl.when(t > 0)
        def _():
            ag_wait(rw(z + t, kp))

        spmm(cnt, tab, rw(z - t, (k + (t + 3) // 4) % 2), rw(z + t, kp), fwd_place)

        @pl.when(t == 3)
        def _():
            ag_wait(rw(z - 4, kp))

        spmm(cnt, tab, up, rw(z + t + 1, (k + (t + 1) // 4) % 2), fwd_place)
        return carry

    lax.fori_loop(0, 4, ag_step, 0)

    def send_a(j):
        return rcopy(sa.at[xm(j)], ra.at[x], sa_s.at[j], sa_r.at[x], col=cl(xm(j), y))

    def send_b(j):
        return rcopy(sb.at[ym(j)], rb.at[y], sb_s.at[j], sb_r.at[y], col=cl(x, ym(j)))

    def emit(i, carry):
        jx, yy = (i // 4) + 1, i % 4
        xx = xm(jx)
        r = pl.ds(pl.multiple_of(cl(xx, yy) * 256, 256), 256)
        sa[xx, yy] = acc[r, 0:128].astype(BF16)
        sb[yy, xx] = acc[r, 128:256].astype(BF16)

        @pl.when((i % 4 == 3) & (i < 12))
        def _():
            send_a(jx).start()

        return carry

    lax.fori_loop(0, 16, emit, 0)

    def start_b(j, carry):
        send_b(j).start()
        return carry

    lax.fori_loop(1, NY, start_b, 0)

    def transpose(i, carry):
        t = cnt[i].T
        cnt_t[i] = t
        rsum[pl.ds(i, 1), :] = jnp.sum(t.astype(F32), axis=0, keepdims=True)
        return carry

    lax.fori_loop(0, SLOTS, transpose, 0)
    line = lax.broadcasted_iota(jnp.int32, (128, 128), 0)
    lane = lax.broadcasted_iota(jnp.int32, (128, 128), 1)
    hot = ((line // 8) * 2 + line % 8 == dkey[...]) & (line % 8 < 2)
    hot = jnp.where(hot, 1.0, 0.0).astype(BF16)
    part_a = jnp.minimum(rsum[...], 256.0)
    part_b = rsum[...] - part_a
    part_deg = jnp.dot(hot, part_a.astype(BF16), preferred_element_type=F32) + jnp.dot(
        hot, part_b.astype(BF16), preferred_element_type=F32
    )
    dg0[...] = part_deg.reshape(NX, NY, 8, 128)

    def send_dx(j):
        return rcopy(dg0.at[xm(j)], dg1.at[x], dgx_s.at[j], dgx_r.at[x], col=cl(xm(j), y))

    def send_dy(j):
        return rcopy(dg2.at[ym(j)], dg3.at[y], dgy_s.at[j], dgy_r.at[y], col=cl(x, ym(j)))

    for j in range(1, NX):
        send_dx(j).start()
    lax.fori_loop(0, 16, zero_acc, 0)
    dg1[x] = dg0[x]
    for j in range(1, NX):
        rcopy(dg1.at[xm(j)], dg1.at[xm(j)], dgx_s.at[j], dgx_r.at[xm(j)], col=me_c).wait_recv()
    dg2[...] = dg1[0] + dg1[1] + dg1[2] + dg1[3]
    for j in range(1, NY):
        send_dy(j).start()

    def send_a2(j):
        return rcopy(s2a.at[ym(j)], r2a.at[y], s2a_s.at[j], s2a_r.at[y], col=cl(x, ym(j)))

    def send_b2(j):
        return rcopy(s2b.at[xm(j)], r2b.at[x], s2b_s.at[j], s2b_r.at[x], col=cl(xm(j), y))

    for j in range(1, NX):
        rcopy(ra.at[xm(j)], ra.at[xm(j)], sa_s.at[j], sa_r.at[xm(j)], col=me_c).wait_recv()

    def sum_a(yy):
        return (
            sa[x, yy].astype(F32)
            + ra[xm(1), yy].astype(F32)
            + ra[xm(2), yy].astype(F32)
            + ra[xm(3), yy].astype(F32)
        )

    def sum_b(xx):
        return (
            sb[y, xx].astype(F32)
            + rb[ym(1), xx].astype(F32)
            + rb[ym(2), xx].astype(F32)
            + rb[ym(3), xx].astype(F32)
        )

    def stage_a2(j, carry):
        s2a[ym(j)] = sum_a(ym(j)).astype(BF16)
        send_a2(j).start()
        return carry

    lax.fori_loop(1, NY, stage_a2, 0)

    for j in range(1, NY):
        rcopy(rb.at[ym(j)], rb.at[ym(j)], sb_s.at[j], sb_r.at[ym(j)], col=me_c).wait_recv()

    def stage_b2(j, carry):
        s2b[xm(j)] = sum_b(xm(j)).astype(BF16)
        send_b2(j).start()
        return carry

    lax.fori_loop(1, NX, stage_b2, 0)
    nsum[:, 0:128] = sum_a(y)
    nsum[:, 128:256] = sum_b(x)

    dg3[y] = dg2[y]
    for j in range(1, NY):
        rcopy(dg3.at[ym(j)], dg3.at[ym(j)], dgy_s.at[j], dgy_r.at[ym(j)], col=me_c).wait_recv()
    degree = dg3[0] + dg3[1] + dg3[2] + dg3[3]
    inv_lane = 1.0 / jnp.sqrt(degree + 1.0)
    eye = line == lane
    inv_col = jnp.concatenate(
        [
            jnp.sum(jnp.where(eye, inv_lane[b : b + 1, :], 0.0), axis=1, keepdims=True)
            for b in range(2)
        ],
        axis=0,
    )

    for j in range(1, NY):
        rcopy(r2a.at[ym(j)], r2a.at[ym(j)], s2a_s.at[j], s2a_r.at[ym(j)], col=me_c).wait_recv()
    nsum[:, 0:128] += (
        r2a[ym(1)].astype(F32) + r2a[ym(2)].astype(F32) + r2a[ym(3)].astype(F32)
    )
    for j in range(1, NX):
        rcopy(r2b.at[xm(j)], r2b.at[xm(j)], s2b_s.at[j], s2b_r.at[xm(j)], col=me_c).wait_recv()
    nsum[:, 128:256] += (
        r2b[xm(1)].astype(F32) + r2b[xm(2)].astype(F32) + r2b[xm(3)].astype(F32)
    )

    agg[...] = (nsum[...] * inv_col).astype(BF16)
    pre = (
        jnp.dot(feat[...], w_self[...], preferred_element_type=F32)
        + jnp.dot(agg[...], w_neigh[...], preferred_element_type=F32)
        + bias[...]
    )
    sig = jax.nn.sigmoid(pre)
    layer_out[...] = (pre * sig).astype(BF16)
    gpre[...] = (cot[...].astype(F32) * sig * (1.0 + pre * (1.0 - sig))).astype(BF16)
    nt = (((1,), (1,)), ((), ()))
    tn = (((0,), (0,)), ((), ()))
    dtab[me_c] = (
        lax.dot_general(gpre[...], w_neigh[...], nt, preferred_element_type=F32) * inv_col
    ).astype(BF16)

    def full_x(j):
        return rcopy(dtab.at[me_c], dtab.at[me_c], df_s.at[j], df_r.at[me_c], col=cl(xm(j), y))

    def full_y(j):
        return rcopy(dtab.at[me_c], dtab.at[me_c], df_s.at[3 + j], df_r.at[me_c], col=cl(x, ym(j)))

    def half_a(jx, jy):
        part = dtab.at[cl(xm(jx), y), :, pl.ds(0, 128)]
        return rcopy(
            part, part, da_s.at[jx * 4 + jy], da_r.at[cl(xm(jx), y)], col=cl(x, ym(jy))
        )

    def half_b(jx, jy):
        part = dtab.at[cl(x, ym(jy)), :, pl.ds(128, 128)]
        return rcopy(
            part, part, db_s.at[jx * 4 + jy], db_r.at[cl(x, ym(jy))], col=cl(xm(jx), y)
        )

    def start_full(j, carry):
        full_x(j).start()
        full_y(j).start()
        return carry

    lax.fori_loop(1, 4, start_full, 0)

    grad_self[...] = lax.dot_general(
        gpre[...], w_self[...], nt, preferred_element_type=F32
    ).astype(BF16)
    gw = lax.dot_general(feat[...], gpre[...], tn, preferred_element_type=F32).astype(BF16)
    ws1[0, 0:128, :] = gw[0:128]
    ws1[1, 0:128, :] = gw[128:256]
    gw = lax.dot_general(agg[...], gpre[...], tn, preferred_element_type=F32).astype(BF16)
    ws1[2, 0:128, :] = gw[0:128]
    ws1[3, 0:128, :] = gw[128:256]
    gb = jnp.broadcast_to(jnp.sum(gpre[...].astype(F32), axis=0, keepdims=True), (16, 256))
    for j in range(4):
        ws1[j, 128:144, :] = gb.astype(BF16)

    def send_w1(j):
        return rcopy(ws1.at[xm(j)], wr1.at[x], w1_s.at[j], w1_r.at[x], col=cl(xm(j), y))

    def send_w2(j):
        return rcopy(ws2.at[ym(j)], wr2.at[y], w2_s.at[j], w2_r.at[y], col=cl(x, ym(j)))

    def send_wp():
        return rcopy(wps, wpr, wp_s, wp_r, row=partner)

    def send_wz(j):
        return rcopy(wz.at[z], wz.at[z], wz_s.at[j], wz_r.at[z], row=rw(z + j, k))

    def send_wy(j):
        return rcopy(wg.at[x, y], wg.at[x, y], wy_s.at[j], wy_r.at[y], col=cl(x, ym(j)))

    def send_wx(j):
        return rcopy(wg.at[x], wg.at[x], wx_s.at[j], wx_r.at[x], col=cl(xm(j), y))

    for j in range(1, NX):
        send_w1(j).start()
    wr1[x] = ws1[x]

    def take_x(jx):
        c = cl(xm(jx), y)
        rcopy(dtab.at[c], dtab.at[c], df_s.at[jx], df_r.at[c], col=me_c).wait_recv()

        def go(jy, carry):
            half_a(jx, jy).start()
            return carry

        lax.fori_loop(1, 4, go, 0)

    def take_y(jy):
        c = cl(x, ym(jy))
        rcopy(dtab.at[c], dtab.at[c], df_s.at[jy], df_r.at[c], col=me_c).wait_recv()

        def go(jx, carry):
            half_b(jx, jy).start()
            return carry

        lax.fori_loop(1, 4, go, 0)

    def take_rest(c):
        part = dtab.at[c, :, pl.ds(0, 128)]
        rcopy(part, part, da_s.at[0], da_r.at[c], col=me_c).wait_recv()
        part = dtab.at[c, :, pl.ds(128, 128)]
        rcopy(part, part, db_s.at[0], db_r.at[c], col=me_c).wait_recv()

    take_x(1)
    take_y(1)
    take_x(3)
    take_y(3)

    def order(q):
        m = q - 7
        dx = jnp.where(q < 4, q, jnp.where(q < 7, 0, 1 + m // 3))
        dy = jnp.where(q < 4, 0, jnp.where(q < 7, q - 3, 1 + m % 3))
        return cl(xm(dx), ym(dy))

    def bwd_step(g, carry):
        @pl.when(g == 1)
        def _():
            take_x(2)
            take_y(2)

        @pl.when(g == 2)
        def _():
            for j in range(1, NX):
                rcopy(wr1.at[xm(j)], wr1.at[xm(j)], w1_s.at[j], w1_r.at[xm(j)], col=me_c).wait_recv()
            tot = (
                wr1[0].astype(F32) + wr1[1].astype(F32) + wr1[2].astype(F32) + wr1[3].astype(F32)
            )
            for j in range(4):
                ws2[j, 0:32, :] = tot[j * 32 : j * 32 + 32]
                ws2[j, 32:40, :] = tot[128:136]
            for j in range(1, NY):
                send_w2(j).start()
            wr2[y] = ws2[y]

        @pl.when(g == 4)
        def _():
            for j in range(1, NY):
                rcopy(wr2.at[ym(j)], wr2.at[ym(j)], w2_s.at[j], w2_r.at[ym(j)], col=me_c).wait_recv()
            wps[...] = wr2[0] + wr2[1] + wr2[2] + wr2[3]
            send_wp().start()

        @pl.when(g == 5)
        def _():
            send_wp().wait_recv()
            wz[z] = wps[...] + wpr[...]
            for j in range(1, NZ):
                send_wz(j).start()

        @pl.when(g == 7)
        def _():
            for j in range(1, NZ):
                zz = zm(z + j)
                rcopy(wz.at[zz], wz.at[zz], wz_s.at[j], wz_r.at[zz], row=me_r).wait_recv()
            tot = wz[0]
            for j in range(1, NZ):
                tot = tot + wz[j]
            g_b[...] = tot[32:33] * scale
            wg[x, y] = tot[0:32]
            for j in range(1, NY):
                send_wy(j).start()

        @pl.when(g > 3)
        def _():
            take_rest(order(2 * g))

        @pl.when(g > 2)
        def _():
            take_rest(order(2 * g + 1))

        spmm(cnt_t, dtab, order(2 * g), order(2 * g + 1), bwd_place)
        return carry

    lax.fori_loop(0, 8, bwd_step, 0)

    def chunk(zz, kk):
        return acc[pl.ds(pl.multiple_of(rw(zz, kk) * 256, 256), 256), :]

    def send_p(zz):
        return rcopy(psend.at[zz], precv.at[zz], p_s.at[zz], p_r.at[zz], row=partner)

    def put_p(zz):
        psend[zz] = chunk(zz, kp).astype(BF16)
        send_p(zz).start()

    def emit_p(t, carry):
        put_p(zm(z + 4 - t))

        @pl.when(t < 3)
        def _():
            put_p(zm(z + 5 + t))

        return carry

    lax.fori_loop(0, 4, emit_p, 0)
    put_p(z)

    def send_u(t):
        return rcopy(usend.at[t], urecv.at[t], u_s.at[t], u_r.at[t], row=rw(z + 1, k))

    def send_d(t):
        return rcopy(dsend.at[t], drecv.at[t], d_s.at[t], d_r.at[t], row=rw(z - 1, k))

    def ring(t, carry):
        zz = zm(z + 4 - t)
        send_p(zz).wait_recv()
        part = chunk(zz, k) + precv[zz].astype(F32)

        @pl.when(t == 0)
        def _():
            usend[t] = part.astype(BF16)

        @pl.when(t > 0)
        def _():
            send_u(t - 1).wait_recv()
            usend[t] = (part + urecv[t - 1].astype(F32)).astype(BF16)

        send_u(t).start()

        @pl.when(t < 3)
        def _():
            zd = zm(z + 5 + t)
            send_p(zd).wait_recv()
            part_d = chunk(zd, k) + precv[zd].astype(F32)

            @pl.when(t == 0)
            def _():
                dsend[t] = part_d.astype(BF16)

            @pl.when(t > 0)
            def _():
                send_d(t - 1).wait_recv()
                dsend[t] = (part_d + drecv[t - 1].astype(F32)).astype(BF16)

            send_d(t).start()

        @pl.when(t == 1)
        def _():
            for j in range(1, NY):
                part_w = wg.at[x, ym(j)]
                rcopy(part_w, part_w, wy_s.at[j], wy_r.at[ym(j)], col=me_c).wait_recv()
            for j in range(1, NX):
                send_wx(j).start()

        return carry

    lax.fori_loop(0, 4, ring, 0)
    send_p(z).wait_recv()

    for j in range(1, NX):
        part_w = wg.at[xm(j)]
        rcopy(part_w, part_w, wx_s.at[j], wx_r.at[xm(j)], col=me_c).wait_recv()
    g_ws[...] = wg[0:2].reshape(256, 256) * scale
    g_wn[...] = wg[2:4].reshape(256, 256) * scale

    for u in range(4):
        ag_up(emb, me_r, u).wait_send()
        send_u(u).wait_send()
    for u in range(3):
        ag_down(emb, me_r, u).wait_send()
        send_d(u).wait_send()
    send_wp().wait_send()

    def drain_z(j, carry):
        ag_partner(emb, j * 2).wait_send()
        send_p(j).wait_send()
        return carry

    lax.fori_loop(0, NZ, drain_z, 0)

    def drain_wz(j, carry):
        send_wz(j).wait_send()
        return carry

    lax.fori_loop(1, NZ, drain_wz, 0)

    def drain_xy(j, carry):
        for copy in (
            send_a(j), send_b(j), send_a2(j), send_b2(j), send_dx(j), send_dy(j), full_x(j), full_y(j),
            send_w1(j), send_w2(j), send_wy(j), send_wx(j),
        ):
            copy.wait_send()
        for i in range(1, 4):
            half_a(j, i).wait_send()
            half_b(j, i).wait_send()
        return carry

    lax.fori_loop(1, 4, drain_xy, 0)

    send_u(3).wait_recv()
    send_d(2).wait_recv()
    grad_source[...] = (
        chunk(z, k) + precv[z].astype(F32) + urecv[3].astype(F32) + drecv[2].astype(F32)
    ).astype(BF16)


def body(
    source_emb, self_feat, w_self, w_neigh, bias, cotangent, tile_dst, tile_src, tile_live, tile_counts
):
    counts = tile_counts.reshape(SLOTS, 128, 128)
    slot = jnp.arange(SLOTS, dtype=jnp.int32)
    used = slot < tile_live.reshape(())
    dst = tile_dst.reshape(SLOTS)
    dkey = jnp.where(used, dst, -1)
    key = jnp.where(used, dst * NB + tile_src.reshape(SLOTS), -1)
    places = jnp.arange(NB * NB, dtype=jnp.int32)
    sel = ZERO_SLOT + jnp.sum(
        jnp.where(places[:, None] == key[None, :], slot[None, :] - ZERO_SLOT, 0), axis=1
    )
    scale = 1.0 / math.sqrt(self_feat.shape[0] * lax.axis_size("row") * lax.axis_size("col"))
    vm = pl.BlockSpec(memory_space=pltpu.VMEM)
    dma = pltpu.SemaphoreType.DMA
    v = pltpu.VMEM
    outs = pl.pallas_call(
        functools.partial(kernel, scale),
        out_shape=(
            jax.ShapeDtypeStruct((256, 256), BF16),
            jax.ShapeDtypeStruct((256, 256), BF16),
            jax.ShapeDtypeStruct((256, 256), BF16),
            jax.ShapeDtypeStruct((256, 256), F32),
            jax.ShapeDtypeStruct((256, 256), F32),
            jax.ShapeDtypeStruct((1, 256), F32),
        ),
        in_specs=[pl.BlockSpec(memory_space=pltpu.SMEM)] + [vm] * 7 + [pl.BlockSpec(memory_space=pl.ANY)],
        out_specs=(vm,) * 6,
        scratch_shapes=[
            v((SLOTS, 128, 128), jnp.int32),
            v((SLOTS + 1, 128, 128), BF16),
            v((SLOTS + 1, 128, 128), BF16),
            v((4096, 256), F32),
            v((16, 256, 256), BF16),
            v((NX, NY, 256, 128), BF16),
            v((NY, NX, 256, 128), BF16),
            v((NX, NY, 256, 128), BF16),
            v((NY, NX, 256, 128), BF16),
            v((NY, 256, 128), BF16),
            v((NX, 256, 128), BF16),
            v((NY, 256, 128), BF16),
            v((NX, 256, 128), BF16),
            v((256, 256), F32),
            v((SLOTS, 128), F32),
            v((NX, NY, 8, 128), F32),
            v((NX, NY, 8, 128), F32),
            v((NY, 8, 128), F32),
            v((NY, 8, 128), F32),
            v((256, 256), BF16),
            v((256, 256), BF16),
            v((16, 256, 256), BF16),
            v((NX, 144, 256), BF16),
            v((NX, 144, 256), BF16),
            v((NY, 40, 256), F32),
            v((NY, 40, 256), F32),
            v((40, 256), F32),
            v((40, 256), F32),
            v((NZ, 40, 256), F32),
            v((NX, NY, 32, 256), F32),
            v((NZ, 256, 256), BF16),
            v((NZ, 256, 256), BF16),
            v((4, 256, 256), BF16),
            v((4, 256, 256), BF16),
            v((3, 256, 256), BF16),
            v((3, 256, 256), BF16),
            dma((16,)),
            dma((16,)),
            dma((4,)),
            dma((3,)),
            dma((NZ,)),
            dma((4,)), dma((4,)),
            dma((4,)), dma((4,)),
            dma((4,)), dma((4,)),
            dma((4,)), dma((4,)),
            dma((4,)), dma((4,)),
            dma((4,)), dma((4,)),
            dma((7,)), dma((16,)),
            dma((16,)), dma((16,)),
            dma((16,)), dma((16,)),
            dma((4,)), dma((4,)),
            dma((4,)), dma((4,)),
            dma, dma,
            dma((NZ,)), dma((NZ,)),
            dma((4,)), dma((4,)),
            dma((4,)), dma((4,)),
            dma((NZ,)), dma((NZ,)),
            dma((4,)), dma((4,)),
            dma((3,)), dma((3,)),
        ],
        compiler_params=pltpu.CompilerParams(
            collective_id=0, has_side_effects=True, vmem_limit_bytes=56 * 1024 * 1024
        ),
    )(
        sel, dkey.reshape(1, SLOTS), source_emb, self_feat, w_self, w_neigh, bias.reshape(1, -1), cotangent, counts
    )
    layer_out, grad_self, grad_source, g_ws, g_wn, g_b = outs
    return layer_out, grad_self, grad_source, g_ws, g_wn, g_b.reshape(-1)


def solution(mesh):
    in_specs = (
        P(("col", "row"), None),
        P(("row", "col"), None),
        P(),
        P(),
        P(),
        P(("row", "col"), None),
        P("row", "col", None),
        P("row", "col", None),
        P("row", "col"),
        P("row", "col", None, None, None),
    )
    out_specs = (
        P(("row", "col"), None),
        P(("row", "col"), None),
        P(("col", "row"), None),
        P(),
        P(),
        P(),
    )
    return jax.shard_map(body, mesh=mesh, in_specs=in_specs, out_specs=out_specs, check_vma=False)
```

```python
import functools
import math

import jax
import jax.numpy as jnp
from jax import lax
from jax.experimental import pallas as pl
from jax.experimental.pallas import tpu as pltpu
from jax.sharding import PartitionSpec as P

F32, BF16 = jnp.float32, jnp.bfloat16
MESH = pl.DeviceIdType.MESH
NZ, NX, NY = 8, 4, 4
NB = 32
SLOTS = 128
ZERO_SLOT = SLOTS


def rcopy(src, dst, ssem, rsem, **where):
    return pltpu.make_async_remote_copy(
        src_ref=src, dst_ref=dst, send_sem=ssem, recv_sem=rsem, device_id=where, device_id_type=MESH
    )


def kernel(
    scale,
    dst_at, src_at, live_at, dst_ids, live, emb, feat, w_self, w_neigh, bias, cot, counts,
    layer_out, grad_self, grad_source, g_ws, g_wn, g_b,
    sel, selv, stage, cnt, cnt_t, acc, tab, sa, sb, ra, rb, s2a, s2b, r2a, r2b, nsum, rsum, dg0, dg1, dg2,
    dg3, agg, gpre, dtab, gwb, gwr, w1s, w1r, wz, x1s, x1r, gfin, psend, precv, esend, e3, e4, f1, f2,
    csem, selsem, ag_r, ag_s, ag_sp, sa_s, sa_r, sb_s, sb_r, s2a_s, s2a_r, s2b_s, s2b_r,
    dgx_s, dgx_r, dgy_s, dgy_r, df_s, df_r, da_s, da_r, db_s, db_r,
    w0_s, w0_r, w1_s, w1_r, w2_s, w2_r, x1_s, x1_r, x2_s, x2_r, pf_s, pf_r,
    p_s, p_r, e3_s, e3_r, e4_s, e4_r, f1_s, f1_r, f2_s, f2_r,
):
    me_r, me_c = lax.axis_index("row"), lax.axis_index("col")
    z, k = me_r // 2, me_r % 2
    x, y = me_c // NY, me_c % NY
    kp = 1 - k

    def zm(v):
        return (v + 2 * NZ) % NZ

    def rw(zz, kk):
        return zm(zz) * 2 + kk

    def xm(j):
        return (x + j) % NX

    def ym(j):
        return (y + j) % NY

    def cl(xx, yy):
        return xx * NY + yy

    partner = rw(z, kp)

    def count_copy(i):
        part = pl.ds(i * 8, 8)
        return pltpu.make_async_copy(counts.at[part], stage.at[part], csem.at[i])

    def start_counts(i, carry):
        count_copy(i).start()
        return carry


    barrier = pltpu.get_barrier_semaphore()

    def greet_z(j, carry):
        pl.semaphore_signal(barrier, inc=1, device_id={"row": rw(z + j, k)}, device_id_type=MESH)
        return carry

    def greet_c(j, carry):
        pl.semaphore_signal(barrier, inc=1, device_id={"col": (me_c + j) % 16}, device_id_type=MESH)
        return carry

    pl.semaphore_signal(barrier, inc=1, device_id={"row": partner}, device_id_type=MESH)
    lax.fori_loop(1, NZ, greet_z, 0)
    lax.fori_loop(1, NX * NY, greet_c, 0)

    line = lax.broadcasted_iota(jnp.int32, (128, 128), 0)
    lane = lax.broadcasted_iota(jnp.int32, (128, 128), 1)
    used = lane < live[...]
    nt = (((1,), (1,)), ((), ()))
    tn = (((0,), (0,)), ((), ()))
    place = line[0:NB] * NB + lane[0:NB]
    in_use = lane[0:NB] < NB
    place = jnp.where(in_use, place, -2)

    def put_slot(i, table):
        for u in range(8):
            s = i * 8 + u
            key = jnp.where(s < live_at[0, 0], dst_at[0, s] * NB + src_at[0, s], -1)
            table = jnp.where(place == key, s, table)
        return table

    selv[...] = lax.fori_loop(
        0, SLOTS // 8, put_slot, jnp.full((NB, 128), ZERO_SLOT, jnp.int32)
    )
    sel_copy = pltpu.make_async_copy(selv, sel, selsem)
    sel_copy.start()
    sel_copy.wait()

    pl.semaphore_wait(barrier, 1 + (NZ - 1) + (NX * NY - 1))

    def shard(r, h):
        return tab.at[r, h]

    def own(h):
        return emb.at[pl.ds(pl.multiple_of(h * 128, 128), 128), :]

    def ag_send(src, r, h, i, dz):
        return rcopy(src, shard(r, h), ag_s.at[i, h], ag_r.at[r, h], row=rw(z + dz, k))

    def ag_partner(src, r, h):
        return rcopy(src, shard(r, h), ag_sp.at[r // 2, h], ag_r.at[r, h], row=partner)

    def ag_wait(r, h):
        rcopy(shard(r, h), shard(r, h), ag_sp.at[r // 2, h], ag_r.at[r, h], row=partner).wait_recv()

    for h in range(2):
        ag_send(own(h), me_r, h, 0, 2).start()
        ag_send(own(h), me_r, h, 1, -2).start()
        ag_send(own(h), me_r, h, 2, 1).start()
        ag_send(own(h), me_r, h, 3, -1).start()
    for h in range(2):
        ag_partner(own(h), me_r, h).start()
    lax.fori_loop(0, 16, start_counts, 0)
    tab[me_r, 0] = emb[0:128]
    tab[me_r, 1] = emb[128:256]
    cnt[ZERO_SLOT] = jnp.zeros((128, 128), BF16)
    cnt_t[ZERO_SLOT] = jnp.zeros((128, 128), BF16)

    def zero_acc(i, carry):
        acc[pl.ds(pl.multiple_of(i * 256, 256), 256), :] = jnp.zeros((256, 256), F32)
        return carry

    lax.fori_loop(0, 16, zero_acc, 0)

    def convert(i, carry):
        count_copy(i).wait()
        part = pl.ds(i * 8, 8)
        cnt[part] = stage[part].astype(F32).astype(BF16)
        return carry

    lax.fori_loop(0, 16, convert, 0)

    def spmm_block(tiles, pick, rhs, b, n, shards):
        rows = []
        for i in range(n):
            parts = []
            for s in shards:
                parts += [tiles[pick(b * n + i, 2 * s)], tiles[pick(b * n + i, 2 * s + 1)]]
            rows.append(jnp.concatenate(parts, axis=1))
        lhs = jnp.concatenate(rows, axis=0)
        r = pl.ds(pl.multiple_of(b * n * 128, n * 128), n * 128)
        acc[r, :] += jnp.dot(
            lhs, jnp.concatenate([rhs(s) for s in shards], axis=0), preferred_element_type=F32
        )

    def spmm(tiles, pick, rhs, shards):
        def block(b, carry):
            spmm_block(tiles, pick, rhs, b, 16, shards)
            return carry

        lax.fori_loop(0, NB // 16, block, 0)

    def source_rows(s):
        return tab[s].reshape(256, 256)

    def grad_rows(s):
        return jnp.concatenate([dtab[s, 0], dtab[s, 1]], axis=1)

    def fwd_pick(d, s):
        return sel[d, s]

    def bwd_pick(s, d):
        return sel[d, s]

    def transpose(i, carry):
        for u in range(4):
            t = cnt[i * 4 + u].T
            cnt_t[i * 4 + u] = t
            rsum[pl.ds(i * 4 + u, 1), :] = jnp.sum(t.astype(F32), axis=0, keepdims=True)
        return carry

    def ag_step(t, carry):
        h = t % 2

        def take(r):
            ag_wait(r, h)
            ag_partner(shard(r, h), r, h).start()

        @pl.when(t < 2)
        def _():
            up, down = rw(z - 2, k), rw(z + 2, k)
            ag_wait(up, h)
            ag_send(shard(up, h), up, h, 4, 1).start()

            @pl.when(h == 0)
            def _():
                ag_send(shard(up, h), up, h, 6, 2).start()

            ag_wait(down, h)
            ag_send(shard(down, h), down, h, 5, -1).start()

            @pl.when(h == 1)
            def _():
                ag_send(shard(down, h), down, h, 6, -2).start()

            ag_partner(shard(up, h), up, h).start()
            ag_partner(shard(down, h), down, h).start()
            take(rw(z - 1, k))
            take(rw(z + 1, k))

        @pl.when(t >= 2)
        def _():
            take(rw(z - 3, k))
            take(rw(z + 3, k))
            take(rw(z + 4, k))

        lax.fori_loop(t * 8, t * 8 + 8, transpose, 0)

        @pl.when(t == 0)
        def _():
            for h in range(2):
                ag_wait(partner, h)

        @pl.when(t == 2)
        def _():
            for h in range(2):
                ag_wait(rw(z - 1, kp), h)
                ag_wait(rw(z + 1, kp), h)

        dz = (t + 1) // 2
        s0 = rw(z - dz, (k + (t // 2) * (3 - t)) % 2)
        s1 = rw(z + dz, (k + (t + 1) % 2) % 2)
        spmm(cnt, fwd_pick, source_rows, (s0, s1))
        return carry

    lax.fori_loop(0, 4, ag_step, 0)

    hot = ((line // 8) * 2 + line % 8 == dst_ids[...]) & (line % 8 < 2) & used
    hot = jnp.where(hot, 1.0, 0.0).astype(BF16)
    part_a = jnp.minimum(rsum[...], 256.0)
    part_b = rsum[...] - part_a
    part_deg = jnp.dot(hot, part_a.astype(BF16), preferred_element_type=F32) + jnp.dot(
        hot, part_b.astype(BF16), preferred_element_type=F32
    )
    dg0[...] = part_deg.reshape(NX, NY, 8, 128)

    def send_dx(j):
        return rcopy(dg0.at[xm(j)], dg1.at[x], dgx_s.at[j], dgx_r.at[x], col=cl(xm(j), y))

    def send_dy(j):
        return rcopy(dg2.at[ym(j)], dg3.at[y], dgy_s.at[j], dgy_r.at[y], col=cl(x, ym(j)))

    for j in range(1, NX):
        send_dx(j).start()
    dg1[x] = dg0[x]

    for h in range(2):
        for dz in (2, 3):
            ag_wait(rw(z - dz, kp), h)
            ag_wait(rw(z + dz, kp), h)
        ag_wait(rw(z - 4, kp), h)

    def send_a(j):
        return rcopy(sa.at[xm(j)], ra.at[x], sa_s.at[j], sa_r.at[x], col=cl(xm(j), y))

    def send_b(jy, xx):
        return rcopy(
            sb.at[ym(jy), xx], rb.at[y, xx], sb_s.at[jy, xx], sb_r.at[y, xx], col=cl(x, ym(jy))
        )

    def emit(jx, carry):
        xx = xm(jx)

        def rest(i, carry):
            shards = ()
            for g in (2 * i, 2 * i + 1):
                dz = 2 + (g + 1) // 2
                shards += (
                    rw(z - dz, (k + (g + 1) % 2) % 2),
                    rw(z + dz, (k + (g + 1) % 2 + g // 3) % 2),
                )
            spmm_block(cnt, fwd_pick, source_rows, xx, 8, shards)
            return carry

        lax.fori_loop(0, 2, rest, 0)

        def put(yy, carry):
            r = pl.ds(pl.multiple_of(cl(xx, yy) * 256, 256), 256)
            sa[xx, yy] = acc[r, 0:128].astype(BF16)
            sb[yy, xx] = acc[r, 128:256].astype(BF16)
            return carry

        lax.fori_loop(0, NY, put, 0)

        @pl.when(jx < 4)
        def _():
            send_a(jx).start()

        for j in range(1, NY):
            send_b(j, xx).start()
        return carry

    lax.fori_loop(1, 5, emit, 0)
    lax.fori_loop(0, 16, zero_acc, 0)
    for j in range(1, NX):
        rcopy(dg1.at[xm(j)], dg1.at[xm(j)], dgx_s.at[j], dgx_r.at[xm(j)], col=me_c).wait_recv()
    dg2[...] = dg1[0] + dg1[1] + dg1[2] + dg1[3]
    for j in range(1, NY):
        send_dy(j).start()

    def send_a2(j):
        return rcopy(s2a.at[ym(j)], r2a.at[y], s2a_s.at[j], s2a_r.at[y], col=cl(x, ym(j)))

    def send_b2(j):
        return rcopy(s2b.at[xm(j)], r2b.at[x], s2b_s.at[j], s2b_r.at[x], col=cl(xm(j), y))

    def sum_a(yy):
        return (
            sa[x, yy].astype(F32)
            + ra[xm(1), yy].astype(F32)
            + ra[xm(2), yy].astype(F32)
            + ra[xm(3), yy].astype(F32)
        )

    def sum_b(xx):
        return (
            sb[y, xx].astype(F32)
            + rb[ym(1), xx].astype(F32)
            + rb[ym(2), xx].astype(F32)
            + rb[ym(3), xx].astype(F32)
        )

    def wait_b(xx):
        for j in range(1, NY):
            part = rb.at[ym(j), xx]
            rcopy(part, part, sb_s.at[j, xx], sb_r.at[ym(j), xx], col=me_c).wait_recv()

    def stage_b2(j, carry):
        wait_b(xm(j))
        s2b[xm(j)] = sum_b(xm(j)).astype(BF16)
        send_b2(j).start()
        return carry

    lax.fori_loop(1, NX, stage_b2, 0)
    for j in range(1, NX):
        rcopy(ra.at[xm(j)], ra.at[xm(j)], sa_s.at[j], sa_r.at[xm(j)], col=me_c).wait_recv()

    def stage_a2(j, carry):
        s2a[ym(j)] = sum_a(ym(j)).astype(BF16)
        send_a2(j).start()
        return carry

    lax.fori_loop(1, NY, stage_a2, 0)
    wait_b(x)
    nsum[:, 0:128] = sum_a(y)
    nsum[:, 128:256] = sum_b(x)

    dg3[y] = dg2[y]
    for j in range(1, NY):
        rcopy(dg3.at[ym(j)], dg3.at[ym(j)], dgy_s.at[j], dgy_r.at[ym(j)], col=me_c).wait_recv()
    degree = dg3[0] + dg3[1] + dg3[2] + dg3[3]
    inv_lane = 1.0 / jnp.sqrt(degree + 1.0)
    eye = line == lane
    inv_col = jnp.concatenate(
        [
            jnp.sum(jnp.where(eye, inv_lane[b : b + 1, :], 0.0), axis=1, keepdims=True)
            for b in range(2)
        ],
        axis=0,
    )

    for j in range(1, NY):
        rcopy(r2a.at[ym(j)], r2a.at[ym(j)], s2a_s.at[j], s2a_r.at[ym(j)], col=me_c).wait_recv()
    nsum[:, 0:128] += (
        r2a[ym(1)].astype(F32) + r2a[ym(2)].astype(F32) + r2a[ym(3)].astype(F32)
    )
    for j in range(1, NX):
        rcopy(r2b.at[xm(j)], r2b.at[xm(j)], s2b_s.at[j], s2b_r.at[xm(j)], col=me_c).wait_recv()
    nsum[:, 128:256] += (
        r2b[xm(1)].astype(F32) + r2b[xm(2)].astype(F32) + r2b[xm(3)].astype(F32)
    )

    agg[...] = (nsum[...] * inv_col).astype(BF16)
    pre = (
        jnp.dot(feat[...], w_self[...], preferred_element_type=F32)
        + jnp.dot(agg[...], w_neigh[...], preferred_element_type=F32)
        + bias[...]
    )
    sig = jax.nn.sigmoid(pre)
    layer_out[...] = (pre * sig).astype(BF16)
    gpre[...] = (cot[...].astype(F32) * sig * (1.0 + pre * (1.0 - sig))).astype(BF16)
    gsum = (
        lax.dot_general(gpre[...], w_neigh[...], nt, preferred_element_type=F32) * inv_col
    ).astype(BF16)
    dtab[me_c, 0] = gsum[:, 0:128]
    dtab[me_c, 1] = gsum[:, 128:256]

    def full_x(j):
        return rcopy(dtab.at[me_c], dtab.at[me_c], df_s.at[j], df_r.at[me_c], col=cl(xm(j), y))

    def full_y(j):
        return rcopy(dtab.at[me_c], dtab.at[me_c], df_s.at[3 + j], df_r.at[me_c], col=cl(x, ym(j)))

    def half_a(jx, jy):
        part = dtab.at[cl(xm(jx), y), 0]
        return rcopy(
            part, part, da_s.at[jx * 4 + jy], da_r.at[cl(xm(jx), y)], col=cl(x, ym(jy))
        )

    def half_b(jx, jy):
        part = dtab.at[cl(x, ym(jy)), 1]
        return rcopy(
            part, part, db_s.at[jx * 4 + jy], db_r.at[cl(x, ym(jy))], col=cl(xm(jx), y)
        )

    def start_full(j, carry):
        full_x(j).start()
        full_y(j).start()
        return carry

    lax.fori_loop(1, 4, start_full, 0)

    grad_self[...] = lax.dot_general(
        gpre[...], w_self[...], nt, preferred_element_type=F32
    ).astype(BF16)
    gwb[0, 0:256, :] = lax.dot_general(feat[...], gpre[...], tn, preferred_element_type=F32)
    gwb[1, 0:256, :] = lax.dot_general(agg[...], gpre[...], tn, preferred_element_type=F32)
    gb = jnp.broadcast_to(jnp.sum(gpre[...].astype(F32), axis=0, keepdims=True), (8, 256))
    gwb[0, 256:264, :] = gb
    gwb[1, 256:264, :] = gb

    def send_w0():
        return rcopy(gwb.at[kp], gwr, w0_s, w0_r, row=partner)

    def send_w1(j):
        zz = zm(z + j)
        return rcopy(w1s.at[zz], w1r.at[z], w1_s.at[j], w1_r.at[z], row=rw(zz, k))

    def send_w2(j):
        return rcopy(wz.at[z], wz.at[z], w2_s.at[j], w2_r.at[z], row=rw(z + j, k))

    def send_x1(j):
        c = (me_c + j) % 16
        return rcopy(x1s.at[c], x1r.at[me_c], x1_s.at[j], x1_r.at[me_c], col=c)

    def send_x2(j):
        part = gfin.at[k, me_c]
        return rcopy(part, part, x2_s.at[j], x2_r.at[me_c], col=(me_c + j) % 16)

    def send_pf():
        return rcopy(gfin.at[k], gfin.at[k], pf_s, pf_r, row=partner)

    send_w0().start()

    def take_x(jx):
        c = cl(xm(jx), y)
        rcopy(dtab.at[c], dtab.at[c], df_s.at[jx], df_r.at[c], col=me_c).wait_recv()

        def go(jy, carry):
            half_a(jx, jy).start()
            return carry

        lax.fori_loop(1, 4, go, 0)

    def take_y(jy):
        c = cl(x, ym(jy))
        rcopy(dtab.at[c], dtab.at[c], df_s.at[jy], df_r.at[c], col=me_c).wait_recv()

        def go(jx, carry):
            half_b(jx, jy).start()
            return carry

        lax.fori_loop(1, 4, go, 0)

    def take_rest(c):
        part = dtab.at[c, 0]
        rcopy(part, part, da_s.at[0], da_r.at[c], col=me_c).wait_recv()
        part = dtab.at[c, 1]
        rcopy(part, part, db_s.at[0], db_r.at[c], col=me_c).wait_recv()

    take_x(1)
    take_y(1)
    take_x(3)
    take_y(3)
    send_w0().wait_recv()
    gwb[k] = gwb[k] + gwr[...]

    def split_z(j, carry):
        w1s[j, 0:32, :] = gwb[k, pl.ds(pl.multiple_of(j * 32, 32), 32), :].astype(BF16)
        w1s[j, 32:48, :] = jnp.concatenate([gwb[k, 256:264, :]] * 2, axis=0).astype(BF16)
        return carry

    lax.fori_loop(0, NZ, split_z, 0)
    for j in range(1, NZ):
        send_w1(j).start()
    w1r[z] = w1s[z]

    def order(q):
        m = q - 7
        dx = jnp.where(q < 4, q, jnp.where(q < 7, 0, 1 + m // 3))
        dy = jnp.where(q < 4, 0, jnp.where(q < 7, q - 3, 1 + m % 3))
        return cl(xm(dx), ym(dy))

    def bwd_step(g, carry):
        @pl.when(g == 1)
        def _():
            take_x(2)
            take_y(2)

        @pl.when(g == 3)
        def _():
            for j in range(1, NZ):
                zz = zm(z + j)
                rcopy(w1r.at[zz], w1r.at[zz], w1_s.at[j], w1_r.at[zz], row=me_r).wait_recv()
            tot = w1r[0].astype(F32)
            for j in range(1, NZ):
                tot = tot + w1r[j].astype(F32)
            wz[z] = tot[0:32]
            gwb[k, 256:264, :] = tot[32:40]
            for j in range(1, NZ):
                send_w2(j).start()

        @pl.when(g > 3)
        def _():
            take_rest(order(2 * g))

        @pl.when(g > 2)
        def _():
            take_rest(order(2 * g + 1))

        spmm(cnt_t, bwd_pick, grad_rows, (order(2 * g), order(2 * g + 1)))
        return carry

    lax.fori_loop(0, 6, bwd_step, 0)
    last = tuple(order(q) for q in range(12, 16))
    for c in last:
        take_rest(c)

    def chunk(zz, kk):
        return acc[pl.ds(pl.multiple_of(rw(zz, kk) * 256, 256), 256), :]

    def send_p(zz):
        return rcopy(psend.at[zz], precv.at[zz], p_s.at[zz], p_r.at[zz], row=partner)

    def put_p(zz):
        psend[zz] = chunk(zz, kp).astype(BF16)
        send_p(zz).start()

    def finish(zz):
        spmm_block(cnt_t, bwd_pick, grad_rows, zz, 4, last)
        put_p(zz)

    def rows_of(h):
        return pl.ds(pl.multiple_of(h * 128, 128), 128)

    def own_part(zz, h):
        r = pl.ds(pl.multiple_of(rw(zz, k) * 256 + h * 128, 128), 128)
        return acc[r, :] + precv[zz, rows_of(h), :].astype(F32)

    def send_e3(i, h):
        return rcopy(
            esend.at[i, h], e3.at[i, h], e3_s.at[i, h], e3_r.at[i, h], row=rw(z + 1 - 2 * i, k)
        )

    def send_e4(i):
        return rcopy(esend.at[2, i], e4.at[i], e4_s.at[i], e4_r.at[i], row=rw(z + 2 - 4 * i, k))

    def send_f1(i, h):
        return rcopy(
            esend.at[3 + i, h], f1.at[i, h], f1_s.at[i, h], f1_r.at[i, h], row=rw(z + 1 - 2 * i, k)
        )

    def send_f2(i, h):
        return rcopy(
            esend.at[5 + i, h], f2.at[i, h], f2_s.at[i, h], f2_r.at[i, h], row=rw(z + 2 - 4 * i, k)
        )

    def finish_at(j, carry):
        dz = (3 + 2 * j) * (j < 2) + 4 * (j == 2) + (2 + 4 * (j - 3)) * ((j > 2) & (j < 5)) + (
            1 + 6 * (j - 5)
        ) * ((j > 4) & (j < 7))
        finish(zm(z + dz))
        return carry

    lax.fori_loop(0, 3, finish_at, 0)

    def first_hop(i, carry):
        zz = zm(z + 3 + 2 * i)
        send_p(zz).wait_recv()
        for h in range(2):
            esend[i, h] = own_part(zz, h).astype(BF16)
            send_e3(i, h).start()
        return carry

    lax.fori_loop(0, 2, first_hop, 0)
    send_p(zm(z + 4)).wait_recv()
    for h in range(2):
        esend[2, h] = own_part(zm(z + 4), h).astype(BF16)
        send_e4(h).start()

    lax.fori_loop(3, 8, finish_at, 0)

    def to_next(i, carry):
        zz = zm(z + 1 + 6 * i)
        send_p(zz).wait_recv()
        for h in range(2):
            esend[3 + i, h] = own_part(zz, h).astype(BF16)
            send_f1(i, h).start()
        return carry

    lax.fori_loop(0, 2, to_next, 0)

    for j in range(1, NZ):
        zz = zm(z + j)
        rcopy(wz.at[zz], wz.at[zz], w2_s.at[j], w2_r.at[zz], row=me_r).wait_recv()

    def split_c(i, carry):
        for u in range(2):
            x1s[2 * i + u, 0:16, :] = wz[i, u * 16 : u * 16 + 16, :]
            x1s[2 * i + u, 16:24, :] = gwb[k, 256:264, :]
        return carry

    lax.fori_loop(0, NZ, split_c, 0)
    x1r[me_c] = x1s[me_c]

    def start_x1(j, carry):
        send_x1(j).start()
        return carry

    lax.fori_loop(1, NX * NY, start_x1, 0)

    def to_second(i, carry):
        zz = zm(z + 2 + 4 * i)
        send_p(zz).wait_recv()
        for h in range(2):
            send_e3(i, h).wait_recv()

            @pl.when(i == h)
            def _():
                send_e4(h).wait_recv()
                esend[5 + i, h] = (
                    own_part(zz, h) + e3[i, h].astype(F32) + e4[h].astype(F32)
                ).astype(BF16)

            @pl.when(i != h)
            def _():
                esend[5 + i, h] = (own_part(zz, h) + e3[i, h].astype(F32)).astype(BF16)

            send_f2(i, h).start()
        return carry

    lax.fori_loop(0, 2, to_second, 0)

    def wait_x1(j, carry):
        c = (me_c + j) % 16
        rcopy(x1r.at[c], x1r.at[c], x1_s.at[j], x1_r.at[c], col=me_c).wait_recv()
        return carry

    lax.fori_loop(1, NX * NY, wait_x1, 0)
    tot = x1r[0]
    for c in range(1, NX * NY):
        tot = tot + x1r[c]
    g_b[...] = tot[16:17] * scale
    gfin[k, me_c] = tot[0:16] * scale

    def start_x2(j, carry):
        send_x2(j).start()
        return carry

    lax.fori_loop(1, NX * NY, start_x2, 0)
    send_p(z).wait_recv()
    for h in range(2):
        for i in range(2):
            send_f1(i, h).wait_recv()
        nsum[h * 128 : h * 128 + 128, :] = (
            own_part(z, h) + f1[0, h].astype(F32) + f1[1, h].astype(F32)
        )

    def wait_x2(j, carry):
        c = (me_c + j) % 16
        part = gfin.at[k, c]
        rcopy(part, part, x2_s.at[j], x2_r.at[c], col=me_c).wait_recv()
        return carry

    lax.fori_loop(1, NX * NY, wait_x2, 0)
    send_pf().start()
    for h in range(2):
        for i in range(2):
            send_f2(i, h).wait_recv()
        grad_source[h * 128 : h * 128 + 128, :] = (
            nsum[h * 128 : h * 128 + 128, :] + f2[0, h].astype(F32) + f2[1, h].astype(F32)
        ).astype(BF16)
    rcopy(gfin.at[kp], gfin.at[kp], pf_s, pf_r, row=partner).wait_recv()
    g_ws[...] = gfin[0].reshape(256, 256)
    g_wn[...] = gfin[1].reshape(256, 256)

    def drain_h(h, carry):
        for i in range(7):
            ag_send(own(h), me_r, h, i, 1).wait_send()
        for j in range(NZ):
            ag_partner(own(h), j * 2, h).wait_send()
        for i in range(2):
            send_e3(i, h).wait_send()
            send_f1(i, h).wait_send()
            send_f2(i, h).wait_send()
        send_e4(h).wait_send()
        return carry

    lax.fori_loop(0, 2, drain_h, 0)
    send_w0().wait_send()
    send_pf().wait_send()
    send_p(0).wait_send()

    def drain_z(j, carry):
        send_p(j).wait_send()
        send_w1(j).wait_send()
        send_w2(j).wait_send()
        return carry

    lax.fori_loop(1, NZ, drain_z, 0)

    def drain_c(j, carry):
        send_x1(j).wait_send()
        send_x2(j).wait_send()
        return carry

    lax.fori_loop(1, NX * NY, drain_c, 0)

    def drain_xy(j, carry):
        for copy in (send_a(j), send_a2(j), send_b2(j), send_dx(j), send_dy(j), full_x(j), full_y(j)):
            copy.wait_send()
        for i in range(1, 4):
            half_a(j, i).wait_send()
            half_b(j, i).wait_send()
        for i in range(4):
            send_b(j, i).wait_send()
        return carry

    lax.fori_loop(1, 4, drain_xy, 0)


def hand_over(*refs):
    n = len(refs) // 2
    for i in range(n):
        refs[n + i][...] = refs[i][...]


def body(
    source_emb, self_feat, w_self, w_neigh, bias, cotangent, tile_dst, tile_src, tile_live, tile_counts
):
    counts = tile_counts.reshape(SLOTS, 128, 128)
    dst, src = tile_dst.reshape(1, SLOTS), tile_src.reshape(1, SLOTS)
    scale = 1.0 / math.sqrt(self_feat.shape[0] * lax.axis_size("row") * lax.axis_size("col"))
    vm = pl.BlockSpec(memory_space=pltpu.VMEM)
    dma = pltpu.SemaphoreType.DMA
    v = pltpu.VMEM
    outs = pl.pallas_call(
        functools.partial(kernel, scale),
        out_shape=(
            jax.ShapeDtypeStruct((256, 256), BF16),
            jax.ShapeDtypeStruct((256, 256), BF16),
            jax.ShapeDtypeStruct((256, 256), BF16),
            jax.ShapeDtypeStruct((256, 256), F32),
            jax.ShapeDtypeStruct((256, 256), F32),
            jax.ShapeDtypeStruct((1, 256), F32),
        ),
        in_specs=[pl.BlockSpec(memory_space=pltpu.SMEM)] * 3 + [vm] * 8 + [pl.BlockSpec(memory_space=pl.ANY)],
        out_specs=(vm,) * 6,
        scratch_shapes=[
            pltpu.SMEM((NB, 128), jnp.int32),
            v((NB, 128), jnp.int32),
            v((SLOTS, 128, 128), jnp.int32),
            v((SLOTS + 1, 128, 128), BF16),
            v((SLOTS + 1, 128, 128), BF16),
            v((4096, 256), F32),
            v((16, 2, 128, 256), BF16),
            v((NX, NY, 256, 128), BF16),
            v((NY, NX, 256, 128), BF16),
            v((NX, NY, 256, 128), BF16),
            v((NY, NX, 256, 128), BF16),
            v((NY, 256, 128), BF16),
            v((NX, 256, 128), BF16),
            v((NY, 256, 128), BF16),
            v((NX, 256, 128), BF16),
            v((256, 256), F32),
            v((SLOTS, 128), F32),
            v((NX, NY, 8, 128), F32),
            v((NX, NY, 8, 128), F32),
            v((NY, 8, 128), F32),
            v((NY, 8, 128), F32),
            v((256, 256), BF16),
            v((256, 256), BF16),
            v((16, 2, 256, 128), BF16),
            v((2, 264, 256), F32),
            v((264, 256), F32),
            v((NZ, 48, 256), BF16),
            v((NZ, 48, 256), BF16),
            v((NZ, 32, 256), F32),
            v((16, 24, 256), F32),
            v((16, 24, 256), F32),
            v((2, 16, 16, 256), F32),
            v((NZ, 256, 256), BF16),
            v((NZ, 256, 256), BF16),
            v((7, 2, 128, 256), BF16),
            v((2, 2, 128, 256), BF16),
            v((2, 128, 256), BF16),
            v((2, 2, 128, 256), BF16),
            v((2, 2, 128, 256), BF16),
            dma((16,)),
            dma,
            dma((16, 2)),
            dma((7, 2)),
            dma((NZ, 2)),
            dma((4,)), dma((4,)),
            dma((4, 4)), dma((4, 4)),
            dma((4,)), dma((4,)),
            dma((4,)), dma((4,)),
            dma((4,)), dma((4,)),
            dma((4,)), dma((4,)),
            dma((7,)), dma((16,)),
            dma((16,)), dma((16,)),
            dma((16,)), dma((16,)),
            dma, dma,
            dma((NZ,)), dma((NZ,)),
            dma((NZ,)), dma((NZ,)),
            dma((16,)), dma((16,)),
            dma((16,)), dma((16,)),
            dma, dma,
            dma((NZ,)), dma((NZ,)),
            dma((2, 2)), dma((2, 2)),
            dma((2,)), dma((2,)),
            dma((2, 2)), dma((2, 2)),
            dma((2, 2)), dma((2, 2)),
        ],
        compiler_params=pltpu.CompilerParams(
            collective_id=0, has_side_effects=True, vmem_limit_bytes=56 * 1024 * 1024
        ),
    )(
        dst, src, tile_live, dst, tile_live,
        source_emb, self_feat, w_self, w_neigh, bias.reshape(1, -1), cotangent, counts,
    )
    outs = pl.pallas_call(
        hand_over,
        out_shape=tuple(jax.ShapeDtypeStruct(o.shape, o.dtype) for o in outs),
        in_specs=[vm] * 6,
        out_specs=(vm,) * 6,
    )(*outs)
    layer_out, grad_self, grad_source, g_ws, g_wn, g_b = outs
    return layer_out, grad_self, grad_source, g_ws, g_wn, g_b.reshape(-1)


def solution(mesh):
    in_specs = (
        P(("col", "row"), None),
        P(("row", "col"), None),
        P(),
        P(),
        P(),
        P(("row", "col"), None),
        P("row", "col", None),
        P("row", "col", None),
        P("row", "col"),
        P("row", "col", None, None, None),
    )
    out_specs = (
        P(("row", "col"), None),
        P(("row", "col"), None),
        P(("col", "row"), None),
        P(),
        P(),
        P(),
    )
    return jax.shard_map(body, mesh=mesh, in_specs=in_specs, out_specs=out_specs, check_vma=False)
```

```python
import functools
import math

import jax
import jax.numpy as jnp
from jax import lax
from jax.experimental import pallas as pl
from jax.experimental.pallas import tpu as pltpu
from jax.sharding import PartitionSpec as P

F32, BF16 = jnp.float32, jnp.bfloat16
MESH = pl.DeviceIdType.MESH
NZ, NX, NY = 8, 4, 4
NB = 32
SLOTS = 128
ZERO_SLOT = SLOTS


def rcopy(src, dst, ssem, rsem, **where):
    return pltpu.make_async_remote_copy(
        src_ref=src, dst_ref=dst, send_sem=ssem, recv_sem=rsem, device_id=where, device_id_type=MESH
    )


def kernel(
    scale,
    dst_at, src_at, live_at, dst_ids, live, emb, feat, w_self, w_neigh, bias, cot, counts,
    layer_out, grad_self, grad_source, g_ws, g_wn, g_b,
    sel, selv, stage, cnt, cnt_t, acc, tab, sa, sb, ra, rb, s2a, s2b, r2a, r2b, nsum, rsum, dg0, dg1, dg2,
    dg3, agg, gpre, dtab, gwb, gwr, w1s, w1r, wz, x1s, x1r, gfin, psend, precv, esend, e3, e4, f1, f2,
    csem, selsem, ag_r, ag_s, ag_sp, sa_s, sa_r, sb_s, sb_r, s2a_s, s2a_r, s2b_s, s2b_r,
    dgx_s, dgx_r, dgy_s, dgy_r, df_s, df_r, da_s, da_r, db_s, db_r,
    w0_s, w0_r, w1_s, w1_r, w2_s, w2_r, x1_s, x1_r, x2_s, x2_r, pf_s, pf_r,
    p_s, p_r, e_s, e3_r, e4_r, f1_r, f2_r,
):
    me_r, me_c = lax.axis_index("row"), lax.axis_index("col")
    z, k = me_r // 2, me_r % 2
    x, y = me_c // NY, me_c % NY
    kp = 1 - k

    def zm(v):
        return (v + 2 * NZ) % NZ

    def rw(zz, kk):
        return zm(zz) * 2 + kk

    def xm(j):
        return (x + j) % NX

    def ym(j):
        return (y + j) % NY

    def cl(xx, yy):
        return xx * NY + yy

    partner = rw(z, kp)

    def count_copy(i):
        part = pl.ds(i * 8, 8)
        return pltpu.make_async_copy(counts.at[part], stage.at[part], csem.at[i])

    def start_counts(i, carry):
        count_copy(i).start()
        return carry


    barrier = pltpu.get_barrier_semaphore()

    def greet_z(j, carry):
        pl.semaphore_signal(barrier, inc=1, device_id={"row": rw(z + j, k)}, device_id_type=MESH)
        return carry

    def greet_c(j, carry):
        pl.semaphore_signal(barrier, inc=1, device_id={"col": (me_c + j) % 16}, device_id_type=MESH)
        return carry

    pl.semaphore_signal(barrier, inc=1, device_id={"row": partner}, device_id_type=MESH)
    lax.fori_loop(1, NZ, greet_z, 0)
    lax.fori_loop(1, NX * NY, greet_c, 0)

    line = lax.broadcasted_iota(jnp.int32, (128, 128), 0)
    lane = lax.broadcasted_iota(jnp.int32, (128, 128), 1)
    used = lane < live[...]
    nt = (((1,), (1,)), ((), ()))
    tn = (((0,), (0,)), ((), ()))
    place = line[0:NB] * NB + lane[0:NB]
    in_use = lane[0:NB] < NB
    place = jnp.where(in_use, place, -2)

    def put_slot(i, table):
        for u in range(8):
            s = i * 8 + u
            key = jnp.where(s < live_at[0, 0], dst_at[0, s] * NB + src_at[0, s], -1)
            table = jnp.where(place == key, s, table)
        return table

    selv[...] = lax.fori_loop(
        0, SLOTS // 8, put_slot, jnp.full((NB, 128), ZERO_SLOT, jnp.int32)
    )
    sel_copy = pltpu.make_async_copy(selv, sel, selsem)
    sel_copy.start()
    sel_copy.wait()

    pl.semaphore_wait(barrier, 1 + (NZ - 1) + (NX * NY - 1))

    def shard(r, h):
        return tab.at[r, h]

    def own(h):
        return emb.at[pl.ds(pl.multiple_of(h * 128, 128), 128), :]

    def ag_send(src, r, h, i, dz):
        return rcopy(src, shard(r, h), ag_s, ag_r.at[r, h], row=rw(z + dz, k))

    def ag_partner(src, r, h):
        return rcopy(src, shard(r, h), ag_sp, ag_r.at[r, h], row=partner)

    def ag_wait(r, h):
        rcopy(shard(r, h), shard(r, h), ag_sp, ag_r.at[r, h], row=partner).wait_recv()

    for h in range(2):
        ag_send(own(h), me_r, h, 0, 2).start()
        ag_send(own(h), me_r, h, 1, -2).start()
        ag_send(own(h), me_r, h, 2, 1).start()
        ag_send(own(h), me_r, h, 3, -1).start()
    for h in range(2):
        ag_partner(own(h), me_r, h).start()
    lax.fori_loop(0, 16, start_counts, 0)
    tab[me_r, 0] = emb[0:128]
    tab[me_r, 1] = emb[128:256]
    cnt[ZERO_SLOT] = jnp.zeros((128, 128), BF16)
    cnt_t[ZERO_SLOT] = jnp.zeros((128, 128), BF16)

    def zero_acc(i, carry):
        acc[pl.ds(pl.multiple_of(i * 256, 256), 256), :] = jnp.zeros((256, 256), F32)
        return carry

    lax.fori_loop(0, 16, zero_acc, 0)

    def convert(i, carry):
        count_copy(i).wait()
        part = pl.ds(i * 8, 8)
        cnt[part] = stage[part].astype(F32).astype(BF16)
        return carry

    lax.fori_loop(0, 16, convert, 0)

    def spmm_block(tiles, pick, rhs, b, n, shards):
        rows = []
        for i in range(n):
            parts = []
            for s in shards:
                parts += [tiles[pick(b * n + i, 2 * s)], tiles[pick(b * n + i, 2 * s + 1)]]
            rows.append(jnp.concatenate(parts, axis=1))
        lhs = jnp.concatenate(rows, axis=0)
        r = pl.ds(pl.multiple_of(b * n * 128, n * 128), n * 128)
        acc[r, :] += jnp.dot(
            lhs, jnp.concatenate([rhs(s) for s in shards], axis=0), preferred_element_type=F32
        )

    def spmm(tiles, pick, rhs, shards):
        def block(b, carry):
            spmm_block(tiles, pick, rhs, b, 16, shards)
            return carry

        lax.fori_loop(0, NB // 16, block, 0)

    def source_rows(s):
        return tab[s].reshape(256, 256)

    def grad_rows(s):
        return jnp.concatenate([dtab[s, 0], dtab[s, 1]], axis=1)

    def fwd_pick(d, s):
        return sel[d, s]

    def bwd_pick(s, d):
        return sel[d, s]

    def transpose(i, carry):
        for u in range(4):
            t = cnt[i * 4 + u].T
            cnt_t[i * 4 + u] = t
            rsum[pl.ds(i * 4 + u, 1), :] = jnp.sum(t.astype(F32), axis=0, keepdims=True)
        return carry

    def ag_step(t, carry):
        h = t % 2

        def take(r):
            ag_wait(r, h)
            ag_partner(shard(r, h), r, h).start()

        @pl.when(t < 2)
        def _():
            up, down = rw(z - 2, k), rw(z + 2, k)
            ag_wait(up, h)
            ag_send(shard(up, h), up, h, 4, 1).start()

            @pl.when(h == 0)
            def _():
                ag_send(shard(up, h), up, h, 6, 2).start()

            ag_wait(down, h)
            ag_send(shard(down, h), down, h, 5, -1).start()

            @pl.when(h == 1)
            def _():
                ag_send(shard(down, h), down, h, 6, -2).start()

            ag_partner(shard(up, h), up, h).start()
            ag_partner(shard(down, h), down, h).start()
            take(rw(z - 1, k))
            take(rw(z + 1, k))

        @pl.when(t >= 2)
        def _():
            take(rw(z - 3, k))
            take(rw(z + 3, k))
            take(rw(z + 4, k))

        lax.fori_loop(t * 8, t * 8 + 8, transpose, 0)

        @pl.when(t == 0)
        def _():
            for h in range(2):
                ag_wait(partner, h)

        @pl.when(t == 2)
        def _():
            for h in range(2):
                ag_wait(rw(z - 1, kp), h)
                ag_wait(rw(z + 1, kp), h)

        dz = (t + 1) // 2
        s0 = rw(z - dz, (k + (t // 2) * (3 - t)) % 2)
        s1 = rw(z + dz, (k + (t + 1) % 2) % 2)
        spmm(cnt, fwd_pick, source_rows, (s0, s1))
        return carry

    lax.fori_loop(0, 4, ag_step, 0)

    hot = ((line // 8) * 2 + line % 8 == dst_ids[...]) & (line % 8 < 2) & used
    hot = jnp.where(hot, 1.0, 0.0).astype(BF16)
    part_a = jnp.minimum(rsum[...], 256.0)
    part_b = rsum[...] - part_a
    part_deg = jnp.dot(hot, part_a.astype(BF16), preferred_element_type=F32) + jnp.dot(
        hot, part_b.astype(BF16), preferred_element_type=F32
    )
    dg0[...] = part_deg.reshape(NX, NY, 8, 128)

    def send_dx(j):
        return rcopy(dg0.at[xm(j)], dg1.at[x], dgx_s, dgx_r, col=cl(xm(j), y))

    def send_dy(j):
        return rcopy(dg2.at[ym(j)], dg3.at[y], dgy_s, dgy_r, col=cl(x, ym(j)))

    for j in range(1, NX):
        send_dx(j).start()
    dg1[x] = dg0[x]

    for h in range(2):
        for dz in (2, 3):
            ag_wait(rw(z - dz, kp), h)
            ag_wait(rw(z + dz, kp), h)
        ag_wait(rw(z - 4, kp), h)

    def send_a(j):
        return rcopy(sa.at[xm(j)], ra.at[x], sa_s, sa_r, col=cl(xm(j), y))

    def send_b(jy, xx):
        return rcopy(
            sb.at[ym(jy), xx], rb.at[y, xx], sb_s, sb_r.at[y, xx], col=cl(x, ym(jy))
        )

    def emit(jx, carry):
        xx = xm(jx)

        def rest(i, carry):
            shards = ()
            for g in (2 * i, 2 * i + 1):
                dz = 2 + (g + 1) // 2
                shards += (
                    rw(z - dz, (k + (g + 1) % 2) % 2),
                    rw(z + dz, (k + (g + 1) % 2 + g // 3) % 2),
                )
            spmm_block(cnt, fwd_pick, source_rows, xx, 8, shards)
            return carry

        lax.fori_loop(0, 2, rest, 0)

        def put(yy, carry):
            r = pl.ds(pl.multiple_of(cl(xx, yy) * 256, 256), 256)
            sa[xx, yy] = acc[r, 0:128].astype(BF16)
            sb[yy, xx] = acc[r, 128:256].astype(BF16)
            return carry

        lax.fori_loop(0, NY, put, 0)

        @pl.when(jx < 4)
        def _():
            send_a(jx).start()

        for j in range(1, NY):
            send_b(j, xx).start()
        return carry

    lax.fori_loop(1, 5, emit, 0)
    lax.fori_loop(0, 16, zero_acc, 0)
    rcopy(dg1.at[0:3], dg1.at[0:3], dgx_s, dgx_r, row=partner).wait_recv()
    dg2[...] = dg1[0] + dg1[1] + dg1[2] + dg1[3]
    for j in range(1, NY):
        send_dy(j).start()

    def send_a2(j):
        return rcopy(s2a.at[ym(j)], r2a.at[y], s2a_s, s2a_r, col=cl(x, ym(j)))

    def send_b2(j):
        return rcopy(s2b.at[xm(j)], r2b.at[x], s2b_s, s2b_r, col=cl(xm(j), y))

    def sum_a(yy):
        return (
            sa[x, yy].astype(F32)
            + ra[xm(1), yy].astype(F32)
            + ra[xm(2), yy].astype(F32)
            + ra[xm(3), yy].astype(F32)
        )

    def sum_b(xx):
        return (
            sb[y, xx].astype(F32)
            + rb[ym(1), xx].astype(F32)
            + rb[ym(2), xx].astype(F32)
            + rb[ym(3), xx].astype(F32)
        )

    def wait_b(xx):
        for j in range(1, NY):
            part = rb.at[ym(j), xx]
            rcopy(part, part, sb_s, sb_r.at[ym(j), xx], col=me_c).wait_recv()

    def stage_b2(j, carry):
        wait_b(xm(j))
        s2b[xm(j)] = sum_b(xm(j)).astype(BF16)
        send_b2(j).start()
        return carry

    lax.fori_loop(1, NX, stage_b2, 0)
    rcopy(ra.at[0:3], ra.at[0:3], sa_s, sa_r, row=partner).wait_recv()

    def stage_a2(j, carry):
        s2a[ym(j)] = sum_a(ym(j)).astype(BF16)
        send_a2(j).start()
        return carry

    lax.fori_loop(1, NY, stage_a2, 0)
    wait_b(x)
    nsum[:, 0:128] = sum_a(y)
    nsum[:, 128:256] = sum_b(x)

    dg3[y] = dg2[y]
    rcopy(dg3.at[0:3], dg3.at[0:3], dgy_s, dgy_r, row=partner).wait_recv()
    degree = dg3[0] + dg3[1] + dg3[2] + dg3[3]
    inv_lane = 1.0 / jnp.sqrt(degree + 1.0)
    eye = line == lane
    inv_col = jnp.concatenate(
        [
            jnp.sum(jnp.where(eye, inv_lane[b : b + 1, :], 0.0), axis=1, keepdims=True)
            for b in range(2)
        ],
        axis=0,
    )

    rcopy(r2a.at[0:3], r2a.at[0:3], s2a_s, s2a_r, row=partner).wait_recv()
    nsum[:, 0:128] += (
        r2a[ym(1)].astype(F32) + r2a[ym(2)].astype(F32) + r2a[ym(3)].astype(F32)
    )
    rcopy(r2b.at[0:3], r2b.at[0:3], s2b_s, s2b_r, row=partner).wait_recv()
    nsum[:, 128:256] += (
        r2b[xm(1)].astype(F32) + r2b[xm(2)].astype(F32) + r2b[xm(3)].astype(F32)
    )

    agg[...] = (nsum[...] * inv_col).astype(BF16)
    pre = (
        jnp.dot(feat[...], w_self[...], preferred_element_type=F32)
        + jnp.dot(agg[...], w_neigh[...], preferred_element_type=F32)
        + bias[...]
    )
    sig = jax.nn.sigmoid(pre)
    layer_out[...] = (pre * sig).astype(BF16)
    gpre[...] = (cot[...].astype(F32) * sig * (1.0 + pre * (1.0 - sig))).astype(BF16)
    gsum = (
        lax.dot_general(gpre[...], w_neigh[...], nt, preferred_element_type=F32) * inv_col
    ).astype(BF16)
    dtab[me_c, 0] = gsum[:, 0:128]
    dtab[me_c, 1] = gsum[:, 128:256]

    def full_x(j):
        return rcopy(dtab.at[me_c], dtab.at[me_c], df_s, df_r.at[me_c], col=cl(xm(j), y))

    def full_y(j):
        return rcopy(dtab.at[me_c], dtab.at[me_c], df_s, df_r.at[me_c], col=cl(x, ym(j)))

    def half_a(jx, jy):
        part = dtab.at[cl(xm(jx), y), 0]
        return rcopy(
            part, part, da_s, da_r.at[cl(xm(jx), y)], col=cl(x, ym(jy))
        )

    def half_b(jx, jy):
        part = dtab.at[cl(x, ym(jy)), 1]
        return rcopy(
            part, part, db_s, db_r.at[cl(x, ym(jy))], col=cl(xm(jx), y)
        )

    def start_full(j, carry):
        full_x(j).start()
        full_y(j).start()
        return carry

    lax.fori_loop(1, 4, start_full, 0)

    grad_self[...] = lax.dot_general(
        gpre[...], w_self[...], nt, preferred_element_type=F32
    ).astype(BF16)
    gwb[0, 0:256, :] = lax.dot_general(feat[...], gpre[...], tn, preferred_element_type=F32)
    gwb[1, 0:256, :] = lax.dot_general(agg[...], gpre[...], tn, preferred_element_type=F32)
    gb = jnp.broadcast_to(jnp.sum(gpre[...].astype(F32), axis=0, keepdims=True), (8, 256))
    gwb[0, 256:264, :] = gb
    gwb[1, 256:264, :] = gb

    def send_w0():
        return rcopy(gwb.at[kp], gwr, w0_s, w0_r, row=partner)

    def send_w1(j):
        zz = zm(z + j)
        return rcopy(w1s.at[zz], w1r.at[z], w1_s, w1_r, row=rw(zz, k))

    def send_w2(j):
        return rcopy(wz.at[z], wz.at[z], w2_s, w2_r, row=rw(z + j, k))

    def send_x1(j):
        c = (me_c + j) % 16
        return rcopy(x1s.at[c], x1r.at[me_c], x1_s, x1_r, col=c)

    def send_x2(j):
        part = gfin.at[k, me_c]
        return rcopy(part, part, x2_s, x2_r, col=(me_c + j) % 16)

    def send_pf():
        return rcopy(gfin.at[k], gfin.at[k], pf_s, pf_r, row=partner)

    send_w0().start()

    def take_x(jx):
        c = cl(xm(jx), y)
        rcopy(dtab.at[c], dtab.at[c], df_s, df_r.at[c], col=me_c).wait_recv()

        def go(jy, carry):
            half_a(jx, jy).start()
            return carry

        lax.fori_loop(1, 4, go, 0)

    def take_y(jy):
        c = cl(x, ym(jy))
        rcopy(dtab.at[c], dtab.at[c], df_s, df_r.at[c], col=me_c).wait_recv()

        def go(jx, carry):
            half_b(jx, jy).start()
            return carry

        lax.fori_loop(1, 4, go, 0)

    def take_rest(c):
        part = dtab.at[c, 0]
        rcopy(part, part, da_s, da_r.at[c], col=me_c).wait_recv()
        part = dtab.at[c, 1]
        rcopy(part, part, db_s, db_r.at[c], col=me_c).wait_recv()

    send_w0().wait_recv()
    gwb[k] = gwb[k] + gwr[...]

    def split_z(j, carry):
        w1s[j, 0:32, :] = gwb[k, pl.ds(pl.multiple_of(j * 32, 32), 32), :].astype(BF16)
        w1s[j, 32:48, :] = jnp.concatenate([gwb[k, 256:264, :]] * 2, axis=0).astype(BF16)
        return carry

    lax.fori_loop(0, NZ, split_z, 0)
    for j in range(1, NZ):
        send_w1(j).start()
    w1r[z] = w1s[z]
    take_x(1)
    take_y(1)
    take_x(3)
    take_y(3)

    def order(q):
        m = q - 7
        dx = jnp.where(q < 4, q, jnp.where(q < 7, 0, 1 + m // 3))
        dy = jnp.where(q < 4, 0, jnp.where(q < 7, q - 3, 1 + m % 3))
        return cl(xm(dx), ym(dy))

    def bwd_step(g, carry):
        @pl.when(g == 1)
        def _():
            take_x(2)
            take_y(2)

        @pl.when(g == 3)
        def _():
            rcopy(w1r.at[0:7], w1r.at[0:7], w1_s, w1_r, row=partner).wait_recv()
            tot = w1r[0].astype(F32)
            for j in range(1, NZ):
                tot = tot + w1r[j].astype(F32)
            wz[z] = tot[0:32]
            gwb[k, 256:264, :] = tot[32:40]
            for j in range(1, NZ):
                send_w2(j).start()

        @pl.when(g > 3)
        def _():
            take_rest(order(2 * g))

        @pl.when(g > 2)
        def _():
            take_rest(order(2 * g + 1))

        spmm(cnt_t, bwd_pick, grad_rows, (order(2 * g), order(2 * g + 1)))
        return carry

    lax.fori_loop(0, 6, bwd_step, 0)
    last = tuple(order(q) for q in range(12, 16))
    for c in last:
        take_rest(c)

    def chunk(zz, kk):
        return acc[pl.ds(pl.multiple_of(rw(zz, kk) * 256, 256), 256), :]

    def send_p(zz):
        return rcopy(psend.at[zz], precv.at[zz], p_s, p_r.at[zz], row=partner)

    def put_p(zz):
        psend[zz] = chunk(zz, kp).astype(BF16)
        send_p(zz).start()

    def finish(zz):
        spmm_block(cnt_t, bwd_pick, grad_rows, zz, 4, last)
        put_p(zz)

    def rows_of(h):
        return pl.ds(pl.multiple_of(h * 128, 128), 128)

    def own_part(zz, h):
        r = pl.ds(pl.multiple_of(rw(zz, k) * 256 + h * 128, 128), 128)
        return acc[r, :] + precv[zz, rows_of(h), :].astype(F32)

    def send_e3(i, h):
        return rcopy(
            esend.at[i, h], e3.at[i, h], e_s, e3_r.at[i, h], row=rw(z + 1 - 2 * i, k)
        )

    def send_e4(i):
        return rcopy(esend.at[2, i], e4.at[i], e_s, e4_r.at[i], row=rw(z + 2 - 4 * i, k))

    def send_f1(i, h):
        return rcopy(
            esend.at[3 + i, h], f1.at[i, h], e_s, f1_r.at[i, h], row=rw(z + 1 - 2 * i, k)
        )

    def send_f2(i, h):
        return rcopy(
            esend.at[5 + i, h], f2.at[i, h], e_s, f2_r.at[i, h], row=rw(z + 2 - 4 * i, k)
        )

    def finish_at(j, carry):
        dz = (3 + 2 * j) * (j < 2) + 4 * (j == 2) + (2 + 4 * (j - 3)) * ((j > 2) & (j < 5)) + (
            1 + 6 * (j - 5)
        ) * ((j > 4) & (j < 7))
        finish(zm(z + dz))
        return carry

    lax.fori_loop(0, 3, finish_at, 0)

    def first_hop(i, carry):
        zz = zm(z + 3 + 2 * i)
        send_p(zz).wait_recv()
        for h in range(2):
            esend[i, h] = own_part(zz, h).astype(BF16)
            send_e3(i, h).start()
        return carry

    lax.fori_loop(0, 2, first_hop, 0)
    send_p(zm(z + 4)).wait_recv()
    for h in range(2):
        esend[2, h] = own_part(zm(z + 4), h).astype(BF16)
        send_e4(h).start()

    lax.fori_loop(3, 8, finish_at, 0)

    def to_next(i, carry):
        zz = zm(z + 1 + 6 * i)
        send_p(zz).wait_recv()
        for h in range(2):
            esend[3 + i, h] = own_part(zz, h).astype(BF16)
            send_f1(i, h).start()
        return carry

    lax.fori_loop(0, 2, to_next, 0)

    rcopy(wz.at[0:7], wz.at[0:7], w2_s, w2_r, row=partner).wait_recv()

    def split_c(i, carry):
        for u in range(2):
            x1s[2 * i + u, 0:16, :] = wz[i, u * 16 : u * 16 + 16, :]
            x1s[2 * i + u, 16:24, :] = gwb[k, 256:264, :]
        return carry

    lax.fori_loop(0, NZ, split_c, 0)
    x1r[me_c] = x1s[me_c]

    def start_x1(j, carry):
        send_x1(j).start()
        return carry

    lax.fori_loop(1, NX * NY, start_x1, 0)

    def to_second(i, carry):
        zz = zm(z + 2 + 4 * i)
        send_p(zz).wait_recv()
        for h in range(2):
            send_e3(i, h).wait_recv()

            @pl.when(i == h)
            def _():
                send_e4(h).wait_recv()
                esend[5 + i, h] = (
                    own_part(zz, h) + e3[i, h].astype(F32) + e4[h].astype(F32)
                ).astype(BF16)

            @pl.when(i != h)
            def _():
                esend[5 + i, h] = (own_part(zz, h) + e3[i, h].astype(F32)).astype(BF16)

            send_f2(i, h).start()
        return carry

    lax.fori_loop(0, 2, to_second, 0)

    rcopy(x1r.at[0:15], x1r.at[0:15], x1_s, x1_r, row=partner).wait_recv()
    tot = x1r[0]
    for c in range(1, NX * NY):
        tot = tot + x1r[c]
    g_b[...] = tot[16:17] * scale
    gfin[k, me_c] = tot[0:16] * scale

    def start_x2(j, carry):
        send_x2(j).start()
        return carry

    lax.fori_loop(1, NX * NY, start_x2, 0)
    send_p(z).wait_recv()
    for h in range(2):
        for i in range(2):
            send_f1(i, h).wait_recv()
        nsum[h * 128 : h * 128 + 128, :] = (
            own_part(z, h) + f1[0, h].astype(F32) + f1[1, h].astype(F32)
        )

    rcopy(gfin.at[k, 0:15], gfin.at[k, 0:15], x2_s, x2_r, row=partner).wait_recv()
    send_pf().start()
    for h in range(2):
        for i in range(2):
            send_f2(i, h).wait_recv()
        grad_source[h * 128 : h * 128 + 128, :] = (
            nsum[h * 128 : h * 128 + 128, :] + f2[0, h].astype(F32) + f2[1, h].astype(F32)
        ).astype(BF16)
    rcopy(gfin.at[kp], gfin.at[kp], pf_s, pf_r, row=partner).wait_recv()
    g_ws[...] = gfin[0].reshape(256, 256)
    g_wn[...] = gfin[1].reshape(256, 256)

    def sent(buf, sem):
        rcopy(buf, buf, sem, ag_r.at[0, 0], row=partner).wait_send()

    sent(tab.at[0:7], ag_s)
    sent(tab.at[0:8], ag_sp)
    sent(sa.at[0:3], sa_s)
    sent(sb.at[0:3], sb_s)
    sent(s2a.at[0:3], s2a_s)
    sent(s2b.at[0:3], s2b_s)
    sent(dg0.at[0:3], dgx_s)
    sent(dg2.at[0:3], dgy_s)
    sent(dtab.at[0:6], df_s)
    sent(dtab.at[0:9, 0], da_s)
    sent(dtab.at[0:9, 1], db_s)
    sent(w1s.at[0:7], w1_s)
    sent(wz.at[0:7], w2_s)
    sent(x1s.at[0:15], x1_s)
    sent(gfin.at[k, 0:15], x2_s)
    sent(psend, p_s)
    sent(esend, e_s)
    send_w0().wait_send()
    send_pf().wait_send()


def hand_over(*refs):
    n = len(refs) // 2
    for i in range(n):
        refs[n + i][...] = refs[i][...]


def body(
    source_emb, self_feat, w_self, w_neigh, bias, cotangent, tile_dst, tile_src, tile_live, tile_counts
):
    counts = tile_counts.reshape(SLOTS, 128, 128)
    dst, src = tile_dst.reshape(1, SLOTS), tile_src.reshape(1, SLOTS)
    scale = 1.0 / math.sqrt(self_feat.shape[0] * lax.axis_size("row") * lax.axis_size("col"))
    vm = pl.BlockSpec(memory_space=pltpu.VMEM)
    dma = pltpu.SemaphoreType.DMA
    v = pltpu.VMEM
    outs = pl.pallas_call(
        functools.partial(kernel, scale),
        out_shape=(
            jax.ShapeDtypeStruct((256, 256), BF16),
            jax.ShapeDtypeStruct((256, 256), BF16),
            jax.ShapeDtypeStruct((256, 256), BF16),
            jax.ShapeDtypeStruct((256, 256), F32),
            jax.ShapeDtypeStruct((256, 256), F32),
            jax.ShapeDtypeStruct((1, 256), F32),
        ),
        in_specs=[pl.BlockSpec(memory_space=pltpu.SMEM)] * 3 + [vm] * 8 + [pl.BlockSpec(memory_space=pl.ANY)],
        out_specs=(vm,) * 6,
        scratch_shapes=[
            pltpu.SMEM((NB, 128), jnp.int32),
            v((NB, 128), jnp.int32),
            v((SLOTS, 128, 128), jnp.int32),
            v((SLOTS + 1, 128, 128), BF16),
            v((SLOTS + 1, 128, 128), BF16),
            v((4096, 256), F32),
            v((16, 2, 128, 256), BF16),
            v((NX, NY, 256, 128), BF16),
            v((NY, NX, 256, 128), BF16),
            v((NX, NY, 256, 128), BF16),
            v((NY, NX, 256, 128), BF16),
            v((NY, 256, 128), BF16),
            v((NX, 256, 128), BF16),
            v((NY, 256, 128), BF16),
            v((NX, 256, 128), BF16),
            v((256, 256), F32),
            v((SLOTS, 128), F32),
            v((NX, NY, 8, 128), F32),
            v((NX, NY, 8, 128), F32),
            v((NY, 8, 128), F32),
            v((NY, 8, 128), F32),
            v((256, 256), BF16),
            v((256, 256), BF16),
            v((16, 2, 256, 128), BF16),
            v((2, 264, 256), F32),
            v((264, 256), F32),
            v((NZ, 48, 256), BF16),
            v((NZ, 48, 256), BF16),
            v((NZ, 32, 256), F32),
            v((16, 24, 256), F32),
            v((16, 24, 256), F32),
            v((2, 16, 16, 256), F32),
            v((NZ, 256, 256), BF16),
            v((NZ, 256, 256), BF16),
            v((7, 2, 128, 256), BF16),
            v((2, 2, 128, 256), BF16),
            v((2, 128, 256), BF16),
            v((2, 2, 128, 256), BF16),
            v((2, 2, 128, 256), BF16),
            dma((16,)),
            dma,
            dma((16, 2)),
            dma,
            dma,
            dma, dma,
            dma, dma((4, 4)),
            dma, dma,
            dma, dma,
            dma, dma,
            dma, dma,
            dma, dma((16,)),
            dma, dma((16,)),
            dma, dma((16,)),
            dma, dma,
            dma, dma,
            dma, dma,
            dma, dma,
            dma, dma,
            dma, dma,
            dma, dma((NZ,)),
            dma,
            dma((2, 2)),
            dma((2,)),
            dma((2, 2)),
            dma((2, 2)),
        ],
        compiler_params=pltpu.CompilerParams(
            collective_id=0, has_side_effects=True, vmem_limit_bytes=56 * 1024 * 1024
        ),
    )(
        dst, src, tile_live, dst, tile_live,
        source_emb, self_feat, w_self, w_neigh, bias.reshape(1, -1), cotangent, counts,
    )
    outs = pl.pallas_call(
        hand_over,
        out_shape=tuple(jax.ShapeDtypeStruct(o.shape, o.dtype) for o in outs),
        in_specs=[vm] * 6,
        out_specs=(vm,) * 6,
    )(*outs)
    layer_out, grad_self, grad_source, g_ws, g_wn, g_b = outs
    return layer_out, grad_self, grad_source, g_ws, g_wn, g_b.reshape(-1)


def solution(mesh):
    in_specs = (
        P(("col", "row"), None),
        P(("row", "col"), None),
        P(),
        P(),
        P(),
        P(("row", "col"), None),
        P("row", "col", None),
        P("row", "col", None),
        P("row", "col"),
        P("row", "col", None, None, None),
    )
    out_specs = (
        P(("row", "col"), None),
        P(("row", "col"), None),
        P(("col", "row"), None),
        P(),
        P(),
        P(),
    )
    return jax.shard_map(body, mesh=mesh, in_specs=in_specs, out_specs=out_specs, check_vma=False)
```

```python
import functools
import math

import jax
import jax.numpy as jnp
from jax import lax
from jax.experimental import pallas as pl
from jax.experimental.pallas import tpu as pltpu
from jax.sharding import PartitionSpec as P

F32, BF16 = jnp.float32, jnp.bfloat16
MESH = pl.DeviceIdType.MESH
NZ, NX, NY = 8, 4, 4
NB = 32
SLOTS = 128
ZERO_SLOT = SLOTS


def rcopy(src, dst, ssem, rsem, **where):
    return pltpu.make_async_remote_copy(
        src_ref=src, dst_ref=dst, send_sem=ssem, recv_sem=rsem, device_id=where, device_id_type=MESH
    )


def kernel(
    scale,
    dst_at, src_at, live_at, dst_ids, live, emb, feat_in, w_self_in, w_neigh_in, bias_in, cot_in, counts,
    layer_out, grad_self, grad_source, g_ws, g_wn, g_b,
    feat, w_self, w_neigh, bias, cot, sel, selv, stage, cnt, cnt_t, acc, tab, sa, sb, ra, rb, s2a, s2b, r2a, r2b, nsum, rsum, dg0, dg1, dg2,
    dg3, agg, gpre, dtab, gwb, gwr, w1s, w1r, wz, x1s, x1r, gfin, psend, precv, esend, e3, e4, f1, f2,
    isem, csem, selsem, ag_r, ag_s, ag_sp, sa_s, sa_r, sb_s, sb_r, s2a_s, s2a_r, s2b_s, s2b_r,
    dgx_s, dgx_r, dgy_s, dgy_r, df_s, df_r, da_s, da_r, db_s, db_r,
    w0_s, w0_r, w1_s, w1_r, w2_s, w2_r, x1_s, x1_r, x2_s, x2_r, pf_s, pf_r,
    p_s, p_r, e_s, e3_r, e4_r, f1_r, f2_r,
):
    me_r, me_c = lax.axis_index("row"), lax.axis_index("col")
    z, k = me_r // 2, me_r % 2
    x, y = me_c // NY, me_c % NY
    kp = 1 - k

    def zm(v):
        return (v + 2 * NZ) % NZ

    def rw(zz, kk):
        return zm(zz) * 2 + kk

    def xm(j):
        return (x + j) % NX

    def ym(j):
        return (y + j) % NY

    def cl(xx, yy):
        return xx * NY + yy

    partner = rw(z, kp)

    def count_copy(i):
        part = pl.ds(i * 8, 8)
        return pltpu.make_async_copy(counts.at[part], stage.at[part], csem.at[i])

    def start_counts(i, carry):
        count_copy(i).start()
        return carry


    barrier = pltpu.get_barrier_semaphore()

    def greet_z(j, carry):
        pl.semaphore_signal(barrier, inc=1, device_id={"row": rw(z + j, k)}, device_id_type=MESH)
        return carry

    def greet_c(j, carry):
        pl.semaphore_signal(barrier, inc=1, device_id={"col": (me_c + j) % 16}, device_id_type=MESH)
        return carry

    pl.semaphore_signal(barrier, inc=1, device_id={"row": partner}, device_id_type=MESH)
    lax.fori_loop(1, NZ, greet_z, 0)
    lax.fori_loop(1, NX * NY, greet_c, 0)

    line = lax.broadcasted_iota(jnp.int32, (128, 128), 0)
    lane = lax.broadcasted_iota(jnp.int32, (128, 128), 1)
    used = lane < live[...]
    nt = (((1,), (1,)), ((), ()))
    tn = (((0,), (0,)), ((), ()))
    place = line[0:NB] * NB + lane[0:NB]
    in_use = lane[0:NB] < NB
    place = jnp.where(in_use, place, -2)

    def put_slot(i, table):
        for u in range(8):
            s = i * 8 + u
            key = jnp.where(s < live_at[0, 0], dst_at[0, s] * NB + src_at[0, s], -1)
            table = jnp.where(place == key, s, table)
        return table

    selv[...] = lax.fori_loop(
        0, SLOTS // 8, put_slot, jnp.full((NB, 128), ZERO_SLOT, jnp.int32)
    )
    sel_copy = pltpu.make_async_copy(selv, sel, selsem)
    sel_copy.start()
    sel_copy.wait()

    pl.semaphore_wait(barrier, 1 + (NZ - 1) + (NX * NY - 1))

    def shard(r, h):
        return tab.at[r, h]

    def own(h):
        return emb.at[pl.ds(pl.multiple_of(h * 128, 128), 128), :]

    def ag_send(src, r, h, i, dz):
        return rcopy(src, shard(r, h), ag_s, ag_r.at[r, h], row=rw(z + dz, k))

    def ag_partner(src, r, h):
        return rcopy(src, shard(r, h), ag_sp, ag_r.at[r, h], row=partner)

    def ag_wait(r, h):
        rcopy(shard(r, h), shard(r, h), ag_sp, ag_r.at[r, h], row=partner).wait_recv()

    for h in range(2):
        ag_send(own(h), me_r, h, 0, 2).start()
        ag_send(own(h), me_r, h, 1, -2).start()
        ag_send(own(h), me_r, h, 2, 1).start()
        ag_send(own(h), me_r, h, 3, -1).start()
    for h in range(2):
        ag_partner(own(h), me_r, h).start()
    lax.fori_loop(0, 16, start_counts, 0)
    inputs = [
        pltpu.make_async_copy(a, b, isem.at[i])
        for i, (a, b) in enumerate(
            ((feat_in, feat), (w_self_in, w_self), (w_neigh_in, w_neigh), (bias_in, bias), (cot_in, cot))
        )
    ]
    for copy in inputs:
        copy.start()
    tab[me_r, 0] = emb[0:128]
    tab[me_r, 1] = emb[128:256]
    cnt[ZERO_SLOT] = jnp.zeros((128, 128), BF16)
    cnt_t[ZERO_SLOT] = jnp.zeros((128, 128), BF16)

    def zero_acc(i, carry):
        acc[pl.ds(pl.multiple_of(i * 256, 256), 256), :] = jnp.zeros((256, 256), F32)
        return carry

    lax.fori_loop(0, 16, zero_acc, 0)

    def convert(i, carry):
        count_copy(i).wait()
        part = pl.ds(i * 8, 8)
        cnt[part] = stage[part].astype(F32).astype(BF16)
        return carry

    lax.fori_loop(0, 16, convert, 0)

    def spmm_block(tiles, pick, rhs, b, n, shards):
        rows = []
        for i in range(n):
            parts = []
            for s in shards:
                parts += [tiles[pick(b * n + i, 2 * s)], tiles[pick(b * n + i, 2 * s + 1)]]
            rows.append(jnp.concatenate(parts, axis=1))
        lhs = jnp.concatenate(rows, axis=0)
        r = pl.ds(pl.multiple_of(b * n * 128, n * 128), n * 128)
        acc[r, :] += jnp.dot(
            lhs, jnp.concatenate([rhs(s) for s in shards], axis=0), preferred_element_type=F32
        )

    def spmm(tiles, pick, rhs, shards):
        def block(b, carry):
            spmm_block(tiles, pick, rhs, b, 16, shards)
            return carry

        lax.fori_loop(0, NB // 16, block, 0)

    def source_rows(s):
        return tab[s].reshape(256, 256)

    def grad_rows(s):
        return jnp.concatenate([dtab[s, 0], dtab[s, 1]], axis=1)

    def fwd_pick(d, s):
        return sel[d, s]

    def bwd_pick(s, d):
        return sel[d, s]

    def transpose(i, carry):
        for u in range(4):
            t = cnt[i * 4 + u].T
            cnt_t[i * 4 + u] = t
            rsum[pl.ds(i * 4 + u, 1), :] = jnp.sum(t.astype(F32), axis=0, keepdims=True)
        return carry

    def ag_step(t, carry):
        h = t % 2

        def take(r):
            ag_wait(r, h)
            ag_partner(shard(r, h), r, h).start()

        @pl.when(t < 2)
        def _():
            up, down = rw(z - 2, k), rw(z + 2, k)
            ag_wait(up, h)
            ag_send(shard(up, h), up, h, 4, 1).start()

            @pl.when(h == 0)
            def _():
                ag_send(shard(up, h), up, h, 6, 2).start()

            ag_wait(down, h)
            ag_send(shard(down, h), down, h, 5, -1).start()

            @pl.when(h == 1)
            def _():
                ag_send(shard(down, h), down, h, 6, -2).start()

            ag_partner(shard(up, h), up, h).start()
            ag_partner(shard(down, h), down, h).start()
            take(rw(z - 1, k))
            take(rw(z + 1, k))

        @pl.when(t == 2)
        def _():
            take(rw(z - 3, k))
            take(rw(z + 3, k))
            take(rw(z + 4, k))

        @pl.when(t < 2)
        def _():
            lax.fori_loop(16 + t * 8, 24 + t * 8, transpose, 0)

        @pl.when(t == 0)
        def _():
            for h in range(2):
                ag_wait(partner, h)

        @pl.when(t == 2)
        def _():
            for h in range(2):
                ag_wait(rw(z - 1, kp), h)
                ag_wait(rw(z + 1, kp), h)

        dz = (t + 1) // 2
        s0 = rw(z - dz, (k + (t // 2) * (3 - t)) % 2)
        s1 = rw(z + dz, (k + (t + 1) % 2) % 2)
        spmm(cnt, fwd_pick, source_rows, (s0, s1))

        @pl.when(t == 3)
        def _():
            take(rw(z - 3, k))
            take(rw(z + 3, k))
            take(rw(z + 4, k))

        return carry

    lax.fori_loop(0, 16, transpose, 0)
    lax.fori_loop(0, 4, ag_step, 0)

    hot = ((line // 8) * 2 + line % 8 == dst_ids[...]) & (line % 8 < 2) & used
    hot = jnp.where(hot, 1.0, 0.0).astype(BF16)
    part_a = jnp.minimum(rsum[...], 256.0)
    part_b = rsum[...] - part_a
    part_deg = jnp.dot(hot, part_a.astype(BF16), preferred_element_type=F32) + jnp.dot(
        hot, part_b.astype(BF16), preferred_element_type=F32
    )
    dg0[...] = part_deg.reshape(NX, NY, 8, 128)

    def send_dx(j):
        return rcopy(dg0.at[xm(j)], dg1.at[x], dgx_s, dgx_r, col=cl(xm(j), y))

    def send_dy(j):
        return rcopy(dg2.at[ym(j)], dg3.at[y], dgy_s, dgy_r, col=cl(x, ym(j)))

    for j in range(1, NX):
        send_dx(j).start()
    dg1[x] = dg0[x]

    for h in range(2):
        for dz in (2, 3):
            ag_wait(rw(z - dz, kp), h)
            ag_wait(rw(z + dz, kp), h)
        ag_wait(rw(z - 4, kp), h)

    def send_a(jx, yy):
        return rcopy(
            sa.at[xm(jx), yy], ra.at[x, yy], sa_s, sa_r.at[x, yy], col=cl(xm(jx), y)
        )

    def send_b(jy, xx):
        return rcopy(
            sb.at[ym(jy), xx], rb.at[y, xx], sb_s, sb_r.at[y, xx], col=cl(x, ym(jy))
        )

    def emit(jx, carry):
        xx = xm(jx)

        def rest(i, carry):
            shards = ()
            for g in (2 * i, 2 * i + 1):
                dz = 2 + (g + 1) // 2
                shards += (
                    rw(z - dz, (k + (g + 1) % 2) % 2),
                    rw(z + dz, (k + (g + 1) % 2 + g // 3) % 2),
                )
            spmm_block(cnt, fwd_pick, source_rows, xx, 8, shards)
            return carry

        lax.fori_loop(0, 2, rest, 0)

        def put(yy, carry):
            r = pl.ds(pl.multiple_of(cl(xx, yy) * 256, 256), 256)
            sa[xx, yy] = acc[r, 0:128].astype(BF16)
            sb[yy, xx] = acc[r, 128:256].astype(BF16)
            return carry

        lax.fori_loop(0, NY, put, 0)

        @pl.when(jx < 4)
        def _():
            for j in range(1, NY + 1):
                send_a(jx, ym(j)).start()

        for j in range(1, NY):
            send_b(j, xx).start()
        return carry

    lax.fori_loop(1, 5, emit, 0)
    lax.fori_loop(0, 16, zero_acc, 0)
    rcopy(dg1.at[0:3], dg1.at[0:3], dgx_s, dgx_r, row=partner).wait_recv()
    dg2[...] = dg1[0] + dg1[1] + dg1[2] + dg1[3]
    for j in range(1, NY):
        send_dy(j).start()

    def send_a2(j):
        return rcopy(s2a.at[ym(j)], r2a.at[y], s2a_s, s2a_r, col=cl(x, ym(j)))

    def send_b2(j):
        return rcopy(s2b.at[xm(j)], r2b.at[x], s2b_s, s2b_r, col=cl(xm(j), y))

    def sum_a(yy):
        return (
            sa[x, yy].astype(F32)
            + ra[xm(1), yy].astype(F32)
            + ra[xm(2), yy].astype(F32)
            + ra[xm(3), yy].astype(F32)
        )

    def sum_b(xx):
        return (
            sb[y, xx].astype(F32)
            + rb[ym(1), xx].astype(F32)
            + rb[ym(2), xx].astype(F32)
            + rb[ym(3), xx].astype(F32)
        )

    def wait_b(xx):
        for j in range(1, NY):
            part = rb.at[ym(j), xx]
            rcopy(part, part, sb_s, sb_r.at[ym(j), xx], col=me_c).wait_recv()

    def stage_b2(j, carry):
        wait_b(xm(j))
        s2b[xm(j)] = sum_b(xm(j)).astype(BF16)
        send_b2(j).start()
        return carry

    lax.fori_loop(1, NX, stage_b2, 0)

    def wait_a(yy):
        for j in range(1, NX):
            part = ra.at[xm(j), yy]
            rcopy(part, part, sa_s, sa_r.at[xm(j), yy], col=me_c).wait_recv()

    def stage_a2(j, carry):
        wait_a(ym(j))
        s2a[ym(j)] = sum_a(ym(j)).astype(BF16)
        send_a2(j).start()
        return carry

    lax.fori_loop(1, NY, stage_a2, 0)
    wait_a(y)
    wait_b(x)
    nsum[:, 0:128] = sum_a(y)
    nsum[:, 128:256] = sum_b(x)

    dg3[y] = dg2[y]
    rcopy(dg3.at[0:3], dg3.at[0:3], dgy_s, dgy_r, row=partner).wait_recv()
    degree = dg3[0] + dg3[1] + dg3[2] + dg3[3]
    inv_lane = 1.0 / jnp.sqrt(degree + 1.0)
    eye = line == lane
    inv_col = jnp.concatenate(
        [
            jnp.sum(jnp.where(eye, inv_lane[b : b + 1, :], 0.0), axis=1, keepdims=True)
            for b in range(2)
        ],
        axis=0,
    )

    rcopy(r2a.at[0:3], r2a.at[0:3], s2a_s, s2a_r, row=partner).wait_recv()
    nsum[:, 0:128] += (
        r2a[ym(1)].astype(F32) + r2a[ym(2)].astype(F32) + r2a[ym(3)].astype(F32)
    )
    rcopy(r2b.at[0:3], r2b.at[0:3], s2b_s, s2b_r, row=partner).wait_recv()
    nsum[:, 128:256] += (
        r2b[xm(1)].astype(F32) + r2b[xm(2)].astype(F32) + r2b[xm(3)].astype(F32)
    )

    for copy in inputs:
        copy.wait()
    agg[...] = (nsum[...] * inv_col).astype(BF16)
    pre = (
        jnp.dot(feat[...], w_self[...], preferred_element_type=F32)
        + jnp.dot(agg[...], w_neigh[...], preferred_element_type=F32)
        + bias[...]
    )
    sig = jax.nn.sigmoid(pre)
    layer_out[...] = (pre * sig).astype(BF16)
    gpre[...] = (cot[...].astype(F32) * sig * (1.0 + pre * (1.0 - sig))).astype(BF16)
    gsum = (
        lax.dot_general(gpre[...], w_neigh[...], nt, preferred_element_type=F32) * inv_col
    ).astype(BF16)
    dtab[me_c, 0] = gsum[:, 0:128]
    dtab[me_c, 1] = gsum[:, 128:256]

    def full_x(j):
        return rcopy(dtab.at[me_c], dtab.at[me_c], df_s, df_r.at[me_c], col=cl(xm(j), y))

    def full_y(j):
        return rcopy(dtab.at[me_c], dtab.at[me_c], df_s, df_r.at[me_c], col=cl(x, ym(j)))

    def half_a(jx, jy):
        part = dtab.at[cl(xm(jx), y), 0]
        return rcopy(
            part, part, da_s, da_r.at[cl(xm(jx), y)], col=cl(x, ym(jy))
        )

    def half_b(jx, jy):
        part = dtab.at[cl(x, ym(jy)), 1]
        return rcopy(
            part, part, db_s, db_r.at[cl(x, ym(jy))], col=cl(xm(jx), y)
        )

    def start_full(j, carry):
        full_x(j).start()
        full_y(j).start()
        return carry

    lax.fori_loop(1, 4, start_full, 0)

    grad_self[...] = lax.dot_general(
        gpre[...], w_self[...], nt, preferred_element_type=F32
    ).astype(BF16)
    gwb[0, 0:256, :] = lax.dot_general(feat[...], gpre[...], tn, preferred_element_type=F32)
    gwb[1, 0:256, :] = lax.dot_general(agg[...], gpre[...], tn, preferred_element_type=F32)
    gb = jnp.broadcast_to(jnp.sum(gpre[...].astype(F32), axis=0, keepdims=True), (8, 256))
    gwb[0, 256:264, :] = gb
    gwb[1, 256:264, :] = gb

    def send_w0():
        return rcopy(gwb.at[kp], gwr, w0_s, w0_r, row=partner)

    def send_w1(j):
        zz = zm(z + j)
        return rcopy(w1s.at[zz], w1r.at[z], w1_s, w1_r, row=rw(zz, k))

    def send_w2(j):
        return rcopy(wz.at[z], wz.at[z], w2_s, w2_r, row=rw(z + j, k))

    def send_x1(j):
        c = (me_c + j) % 16
        return rcopy(x1s.at[c], x1r.at[me_c], x1_s, x1_r, col=c)

    def send_x2(j):
        part = gfin.at[k, me_c]
        return rcopy(part, part, x2_s, x2_r, col=(me_c + j) % 16)

    def send_pf():
        return rcopy(gfin.at[k], gfin.at[k], pf_s, pf_r, row=partner)

    send_w0().start()

    def take_x(jx):
        c = cl(xm(jx), y)
        rcopy(dtab.at[c], dtab.at[c], df_s, df_r.at[c], col=me_c).wait_recv()

        def go(jy, carry):
            half_a(jx, jy).start()
            return carry

        lax.fori_loop(1, 4, go, 0)

    def take_y(jy):
        c = cl(x, ym(jy))
        rcopy(dtab.at[c], dtab.at[c], df_s, df_r.at[c], col=me_c).wait_recv()

        def go(jx, carry):
            half_b(jx, jy).start()
            return carry

        lax.fori_loop(1, 4, go, 0)

    def take_rest(c):
        part = dtab.at[c, 0]
        rcopy(part, part, da_s, da_r.at[c], col=me_c).wait_recv()
        part = dtab.at[c, 1]
        rcopy(part, part, db_s, db_r.at[c], col=me_c).wait_recv()

    send_w0().wait_recv()
    gwb[k] = gwb[k] + gwr[...]

    def split_z(j, carry):
        w1s[j, 0:32, :] = gwb[k, pl.ds(pl.multiple_of(j * 32, 32), 32), :].astype(BF16)
        w1s[j, 32:48, :] = jnp.concatenate([gwb[k, 256:264, :]] * 2, axis=0).astype(BF16)
        return carry

    lax.fori_loop(0, NZ, split_z, 0)
    for j in range(1, NZ):
        send_w1(j).start()
    w1r[z] = w1s[z]
    take_x(1)
    take_y(1)
    take_x(3)
    take_y(3)

    def order(q):
        m = q - 7
        dx = jnp.where(q < 4, q, jnp.where(q < 7, 0, 1 + m // 3))
        dy = jnp.where(q < 4, 0, jnp.where(q < 7, q - 3, 1 + m % 3))
        return cl(xm(dx), ym(dy))

    def bwd_step(g, carry):
        @pl.when(g == 1)
        def _():
            take_x(2)
            take_y(2)

        @pl.when(g == 3)
        def _():
            rcopy(w1r.at[0:7], w1r.at[0:7], w1_s, w1_r, row=partner).wait_recv()
            tot = w1r[0].astype(F32)
            for j in range(1, NZ):
                tot = tot + w1r[j].astype(F32)
            wz[z] = tot[0:32]
            gwb[k, 256:264, :] = tot[32:40]
            for j in range(1, NZ):
                send_w2(j).start()

        @pl.when(g > 3)
        def _():
            take_rest(order(2 * g))

        @pl.when(g > 2)
        def _():
            take_rest(order(2 * g + 1))

        spmm(cnt_t, bwd_pick, grad_rows, (order(2 * g), order(2 * g + 1)))
        return carry

    lax.fori_loop(0, 6, bwd_step, 0)
    last = tuple(order(q) for q in range(12, 16))
    for c in last:
        take_rest(c)

    def chunk(zz, kk):
        return acc[pl.ds(pl.multiple_of(rw(zz, kk) * 256, 256), 256), :]

    def send_p(zz):
        return rcopy(psend.at[zz], precv.at[zz], p_s, p_r.at[zz], row=partner)

    def put_p(zz):
        psend[zz] = chunk(zz, kp).astype(BF16)
        send_p(zz).start()

    def finish(zz):
        spmm_block(cnt_t, bwd_pick, grad_rows, zz, 4, last)
        put_p(zz)

    def rows_of(h):
        return pl.ds(pl.multiple_of(h * 128, 128), 128)

    def own_part(zz, h):
        r = pl.ds(pl.multiple_of(rw(zz, k) * 256 + h * 128, 128), 128)
        return acc[r, :] + precv[zz, rows_of(h), :].astype(F32)

    def send_e3(i, h):
        return rcopy(
            esend.at[i, h], e3.at[i, h], e_s, e3_r.at[i, h], row=rw(z + 1 - 2 * i, k)
        )

    def send_e4(i):
        return rcopy(esend.at[2, i], e4.at[i], e_s, e4_r.at[i], row=rw(z + 2 - 4 * i, k))

    def send_f1(i, h):
        return rcopy(
            esend.at[3 + i, h], f1.at[i, h], e_s, f1_r.at[i, h], row=rw(z + 1 - 2 * i, k)
        )

    def send_f2(i, h):
        return rcopy(
            esend.at[5 + i, h], f2.at[i, h], e_s, f2_r.at[i, h], row=rw(z + 2 - 4 * i, k)
        )

    def finish_at(j, carry):
        dz = (3 + 2 * j) * (j < 2) + 4 * (j == 2) + (2 + 4 * (j - 3)) * ((j > 2) & (j < 5)) + (
            1 + 6 * (j - 5)
        ) * ((j > 4) & (j < 7))
        finish(zm(z + dz))
        return carry

    lax.fori_loop(0, 3, finish_at, 0)

    def first_hop(i, carry):
        zz = zm(z + 3 + 2 * i)
        send_p(zz).wait_recv()
        for h in range(2):
            esend[i, h] = own_part(zz, h).astype(BF16)
            send_e3(i, h).start()
        return carry

    lax.fori_loop(0, 2, first_hop, 0)
    send_p(zm(z + 4)).wait_recv()
    for h in range(2):
        esend[2, h] = own_part(zm(z + 4), h).astype(BF16)
        send_e4(h).start()

    lax.fori_loop(3, 8, finish_at, 0)

    def to_next(i, carry):
        zz = zm(z + 1 + 6 * i)
        send_p(zz).wait_recv()
        for h in range(2):
            esend[3 + i, h] = own_part(zz, h).astype(BF16)
            send_f1(i, h).start()
        return carry

    lax.fori_loop(0, 2, to_next, 0)

    rcopy(wz.at[0:7], wz.at[0:7], w2_s, w2_r, row=partner).wait_recv()

    def split_c(i, carry):
        for u in range(2):
            x1s[2 * i + u, 0:16, :] = wz[i, u * 16 : u * 16 + 16, :]
            x1s[2 * i + u, 16:24, :] = gwb[k, 256:264, :]
        return carry

    lax.fori_loop(0, NZ, split_c, 0)
    x1r[me_c] = x1s[me_c]

    def start_x1(j, carry):
        send_x1(j).start()
        return carry

    lax.fori_loop(1, NX * NY, start_x1, 0)

    def to_second(i, carry):
        zz = zm(z + 2 + 4 * i)
        send_p(zz).wait_recv()
        for h in range(2):
            send_e3(i, h).wait_recv()

            @pl.when(i == h)
            def _():
                send_e4(h).wait_recv()
                esend[5 + i, h] = (
                    own_part(zz, h) + e3[i, h].astype(F32) + e4[h].astype(F32)
                ).astype(BF16)

            @pl.when(i != h)
            def _():
                esend[5 + i, h] = (own_part(zz, h) + e3[i, h].astype(F32)).astype(BF16)

            send_f2(i, h).start()
        return carry

    lax.fori_loop(0, 2, to_second, 0)

    rcopy(x1r.at[0:15], x1r.at[0:15], x1_s, x1_r, row=partner).wait_recv()
    tot = x1r[0]
    for c in range(1, NX * NY):
        tot = tot + x1r[c]
    g_b[...] = tot[16:17] * scale
    gfin[k, me_c] = tot[0:16] * scale

    def start_x2(j, carry):
        send_x2(j).start()
        return carry

    lax.fori_loop(1, NX * NY, start_x2, 0)
    send_p(z).wait_recv()
    for h in range(2):
        for i in range(2):
            send_f1(i, h).wait_recv()
        nsum[h * 128 : h * 128 + 128, :] = (
            own_part(z, h) + f1[0, h].astype(F32) + f1[1, h].astype(F32)
        )

    rcopy(gfin.at[k, 0:15], gfin.at[k, 0:15], x2_s, x2_r, row=partner).wait_recv()
    send_pf().start()
    for h in range(2):
        for i in range(2):
            send_f2(i, h).wait_recv()
        grad_source[h * 128 : h * 128 + 128, :] = (
            nsum[h * 128 : h * 128 + 128, :] + f2[0, h].astype(F32) + f2[1, h].astype(F32)
        ).astype(BF16)
    rcopy(gfin.at[kp], gfin.at[kp], pf_s, pf_r, row=partner).wait_recv()
    g_ws[...] = gfin[0].reshape(256, 256)
    g_wn[...] = gfin[1].reshape(256, 256)

    def sent(buf, sem):
        rcopy(buf, buf, sem, ag_r.at[0, 0], row=partner).wait_send()

    sent(tab.at[0:7], ag_s)
    sent(tab.at[0:8], ag_sp)
    sent(sa.at[0:3], sa_s)
    sent(sb.at[0:3], sb_s)
    sent(s2a.at[0:3], s2a_s)
    sent(s2b.at[0:3], s2b_s)
    sent(dg0.at[0:3], dgx_s)
    sent(dg2.at[0:3], dgy_s)
    sent(dtab.at[0:6], df_s)
    sent(dtab.at[0:9, 0], da_s)
    sent(dtab.at[0:9, 1], db_s)
    sent(w1s.at[0:7], w1_s)
    sent(wz.at[0:7], w2_s)
    sent(x1s.at[0:15], x1_s)
    sent(gfin.at[k, 0:15], x2_s)
    sent(psend, p_s)
    sent(esend, e_s)
    send_w0().wait_send()
    send_pf().wait_send()


def hand_over(*refs):
    n = len(refs) // 2
    for i in range(n):
        refs[n + i][...] = refs[i][...]


def body(
    source_emb, self_feat, w_self, w_neigh, bias, cotangent, tile_dst, tile_src, tile_live, tile_counts
):
    counts = tile_counts.reshape(SLOTS, 128, 128)
    dst, src = tile_dst.reshape(1, SLOTS), tile_src.reshape(1, SLOTS)
    scale = 1.0 / math.sqrt(self_feat.shape[0] * lax.axis_size("row") * lax.axis_size("col"))
    vm = pl.BlockSpec(memory_space=pltpu.VMEM)
    dma = pltpu.SemaphoreType.DMA
    v = pltpu.VMEM
    outs = pl.pallas_call(
        functools.partial(kernel, scale),
        out_shape=(
            jax.ShapeDtypeStruct((256, 256), BF16),
            jax.ShapeDtypeStruct((256, 256), BF16),
            jax.ShapeDtypeStruct((256, 256), BF16),
            jax.ShapeDtypeStruct((256, 256), F32),
            jax.ShapeDtypeStruct((256, 256), F32),
            jax.ShapeDtypeStruct((1, 256), F32),
        ),
        in_specs=[pl.BlockSpec(memory_space=pltpu.SMEM)] * 3 + [vm] * 3 + [pl.BlockSpec(memory_space=pl.ANY)] * 6,
        out_specs=(vm,) * 6,
        scratch_shapes=[
            v((256, 256), BF16),
            v((256, 256), BF16),
            v((256, 256), BF16),
            v((1, 256), F32),
            v((256, 256), BF16),
            pltpu.SMEM((NB, 128), jnp.int32),
            v((NB, 128), jnp.int32),
            v((SLOTS, 128, 128), jnp.int32),
            v((SLOTS + 1, 128, 128), BF16),
            v((SLOTS + 1, 128, 128), BF16),
            v((4096, 256), F32),
            v((16, 2, 128, 256), BF16),
            v((NX, NY, 256, 128), BF16),
            v((NY, NX, 256, 128), BF16),
            v((NX, NY, 256, 128), BF16),
            v((NY, NX, 256, 128), BF16),
            v((NY, 256, 128), BF16),
            v((NX, 256, 128), BF16),
            v((NY, 256, 128), BF16),
            v((NX, 256, 128), BF16),
            v((256, 256), F32),
            v((SLOTS, 128), F32),
            v((NX, NY, 8, 128), F32),
            v((NX, NY, 8, 128), F32),
            v((NY, 8, 128), F32),
            v((NY, 8, 128), F32),
            v((256, 256), BF16),
            v((256, 256), BF16),
            v((16, 2, 256, 128), BF16),
            v((2, 264, 256), F32),
            v((264, 256), F32),
            v((NZ, 48, 256), BF16),
            v((NZ, 48, 256), BF16),
            v((NZ, 32, 256), F32),
            v((16, 24, 256), F32),
            v((16, 24, 256), F32),
            v((2, 16, 16, 256), F32),
            v((NZ, 256, 256), BF16),
            v((NZ, 256, 256), BF16),
            v((7, 2, 128, 256), BF16),
            v((2, 2, 128, 256), BF16),
            v((2, 128, 256), BF16),
            v((2, 2, 128, 256), BF16),
            v((2, 2, 128, 256), BF16),
            dma((5,)),
            dma((16,)),
            dma,
            dma((16, 2)),
            dma,
            dma,
            dma, dma((4, 4)),
            dma, dma((4, 4)),
            dma, dma,
            dma, dma,
            dma, dma,
            dma, dma,
            dma, dma((16,)),
            dma, dma((16,)),
            dma, dma((16,)),
            dma, dma,
            dma, dma,
            dma, dma,
            dma, dma,
            dma, dma,
            dma, dma,
            dma, dma((NZ,)),
            dma,
            dma((2, 2)),
            dma((2,)),
            dma((2, 2)),
            dma((2, 2)),
        ],
        compiler_params=pltpu.CompilerParams(
            collective_id=0, has_side_effects=True, vmem_limit_bytes=56 * 1024 * 1024
        ),
    )(
        dst, src, tile_live, dst, tile_live,
        source_emb, self_feat, w_self, w_neigh, bias.reshape(1, -1), cotangent, counts,
    )
    outs = pl.pallas_call(
        hand_over,
        out_shape=tuple(jax.ShapeDtypeStruct(o.shape, o.dtype) for o in outs),
        in_specs=[vm] * 6,
        out_specs=(vm,) * 6,
    )(*outs)
    layer_out, grad_self, grad_source, g_ws, g_wn, g_b = outs
    return layer_out, grad_self, grad_source, g_ws, g_wn, g_b.reshape(-1)


def solution(mesh):
    in_specs = (
        P(("col", "row"), None),
        P(("row", "col"), None),
        P(),
        P(),
        P(),
        P(("row", "col"), None),
        P("row", "col", None),
        P("row", "col", None),
        P("row", "col"),
        P("row", "col", None, None, None),
    )
    out_specs = (
        P(("row", "col"), None),
        P(("row", "col"), None),
        P(("col", "row"), None),
        P(),
        P(),
        P(),
    )
    return jax.shard_map(body, mesh=mesh, in_specs=in_specs, out_specs=out_specs, check_vma=False)
```

```python
import functools
import math

import jax
import jax.numpy as jnp
from jax import lax
from jax.experimental import pallas as pl
from jax.experimental.pallas import tpu as pltpu
from jax.sharding import PartitionSpec as P

F32, BF16 = jnp.float32, jnp.bfloat16
MESH = pl.DeviceIdType.MESH
NZ, NX, NY = 8, 4, 4
NB = 32
SLOTS = 128
ZERO_SLOT = SLOTS


def rcopy(src, dst, ssem, rsem, **where):
    return pltpu.make_async_remote_copy(
        src_ref=src, dst_ref=dst, send_sem=ssem, recv_sem=rsem, device_id=where, device_id_type=MESH
    )


def kernel(
    scale,
    dst_at, src_at, live_at, dst_ids, live, emb, feat_in, w_self_in, w_neigh_in, bias_in, cot_in, counts,
    layer_out, grad_self, grad_source, g_ws, g_wn, g_b,
    feat, w_self, w_neigh, bias, cot, sel, selv, stage, cnt, cnt_t, acc, tab, sa, sb, ra, rb, s2a, s2b, r2a, r2b, nsum, rsum, dg0, dg1, dg2,
    dg3, agg, gpre, dtab, gwb, gwr, w1s, w1r, wz, x1s, x1r, gfin, psend, precv, esend, e3, e4, f1, f2,
    isem, csem, selsem, ag_r, ag_s, ag_sp, sa_s, sa_r, sb_s, sb_r, s2a_s, s2a_r, s2b_s, s2b_r,
    dgx_s, dgx_r, dgy_s, dgy_r, df_s, df_r, da_s, da_r, db_s, db_r,
    w0_s, w0_r, w1_s, w1_r, w2_s, w2_r, x1_s, x1_r, x2_s, x2_r, pf_s, pf_r,
    p_s, p_r, e_s, e3_r, e4_r, f1_r, f2_r,
):
    me_r, me_c = lax.axis_index("row"), lax.axis_index("col")
    z, k = me_r // 2, me_r % 2
    x, y = me_c // NY, me_c % NY
    kp = 1 - k

    def zm(v):
        return (v + 2 * NZ) % NZ

    def rw(zz, kk):
        return zm(zz) * 2 + kk

    def xm(j):
        return (x + j) % NX

    def ym(j):
        return (y + j) % NY

    def cl(xx, yy):
        return xx * NY + yy

    partner = rw(z, kp)

    def count_copy(i):
        part = pl.ds(i * 8, 8)
        return pltpu.make_async_copy(counts.at[part], stage.at[part], csem.at[i])

    def start_counts(i, carry):
        count_copy(i).start()
        return carry


    barrier = pltpu.get_barrier_semaphore()

    def greet_z(j, carry):
        pl.semaphore_signal(barrier, inc=1, device_id={"row": rw(z + j, k)}, device_id_type=MESH)
        return carry

    def greet_c(j, carry):
        pl.semaphore_signal(barrier, inc=1, device_id={"col": (me_c + j) % 16}, device_id_type=MESH)
        return carry

    pl.semaphore_signal(barrier, inc=1, device_id={"row": partner}, device_id_type=MESH)
    lax.fori_loop(1, NZ, greet_z, 0)
    lax.fori_loop(1, NX * NY, greet_c, 0)

    line = lax.broadcasted_iota(jnp.int32, (128, 128), 0)
    lane = lax.broadcasted_iota(jnp.int32, (128, 128), 1)
    used = lane < live[...]
    nt = (((1,), (1,)), ((), ()))
    tn = (((0,), (0,)), ((), ()))
    place = line[0:NB] * NB + lane[0:NB]
    in_use = lane[0:NB] < NB
    place = jnp.where(in_use, place, -2)

    def put_slot(i, table):
        for u in range(8):
            s = i * 8 + u
            key = jnp.where(s < live_at[0, 0], dst_at[0, s] * NB + src_at[0, s], -1)
            table = jnp.where(place == key, s, table)
        return table

    selv[...] = lax.fori_loop(
        0, SLOTS // 8, put_slot, jnp.full((NB, 128), ZERO_SLOT, jnp.int32)
    )
    sel_copy = pltpu.make_async_copy(selv, sel, selsem)
    sel_copy.start()
    sel_copy.wait()

    pl.semaphore_wait(barrier, 1 + (NZ - 1) + (NX * NY - 1))

    def shard(r, h):
        return tab.at[r, h]

    def own(h):
        return emb.at[pl.ds(pl.multiple_of(h * 128, 128), 128), :]

    def ag_send(src, r, h, i, dz):
        return rcopy(src, shard(r, h), ag_s, ag_r.at[r, h], row=rw(z + dz, k))

    def ag_partner(src, r, h):
        return rcopy(src, shard(r, h), ag_sp, ag_r.at[r, h], row=partner)

    def ag_wait(r, h):
        rcopy(shard(r, h), shard(r, h), ag_sp, ag_r.at[r, h], row=partner).wait_recv()

    for h in range(2):
        ag_send(own(h), me_r, h, 0, 2).start()
        ag_send(own(h), me_r, h, 1, -2).start()
        ag_send(own(h), me_r, h, 2, 1).start()
        ag_send(own(h), me_r, h, 3, -1).start()
    for h in range(2):
        ag_partner(own(h), me_r, h).start()
    lax.fori_loop(0, 16, start_counts, 0)
    inputs = [
        pltpu.make_async_copy(a, b, isem.at[i])
        for i, (a, b) in enumerate(
            ((feat_in, feat), (w_self_in, w_self), (w_neigh_in, w_neigh), (bias_in, bias), (cot_in, cot))
        )
    ]
    for copy in inputs:
        copy.start()
    tab[me_r, 0] = emb[0:128]
    tab[me_r, 1] = emb[128:256]
    cnt[ZERO_SLOT] = jnp.zeros((128, 128), BF16)
    cnt_t[ZERO_SLOT] = jnp.zeros((128, 128), BF16)

    def zero_acc(i, carry):
        acc[pl.ds(pl.multiple_of(i * 256, 256), 256), :] = jnp.zeros((256, 256), F32)
        return carry

    lax.fori_loop(0, 16, zero_acc, 0)

    def convert(i, carry):
        count_copy(i).wait()
        part = pl.ds(i * 8, 8)
        cnt[part] = stage[part].astype(F32).astype(BF16)
        return carry

    lax.fori_loop(0, 16, convert, 0)

    def spmm_block(tiles, pick, rhs, b, n, shards):
        rows = []
        for i in range(n):
            parts = []
            for s in shards:
                parts += [tiles[pick(b * n + i, 2 * s)], tiles[pick(b * n + i, 2 * s + 1)]]
            rows.append(jnp.concatenate(parts, axis=1))
        lhs = jnp.concatenate(rows, axis=0)
        r = pl.ds(pl.multiple_of(b * n * 128, n * 128), n * 128)
        acc[r, :] += jnp.dot(
            lhs, jnp.concatenate([rhs(s) for s in shards], axis=0), preferred_element_type=F32
        )

    def spmm(tiles, pick, rhs, shards):
        def block(b, carry):
            spmm_block(tiles, pick, rhs, b, 16, shards)
            return carry

        lax.fori_loop(0, NB // 16, block, 0)

    def source_rows(s):
        return tab[s].reshape(256, 256)

    def grad_rows(s):
        return jnp.concatenate([dtab[s, 0], dtab[s, 1]], axis=1)

    def fwd_pick(d, s):
        return sel[d, s]

    def bwd_pick(s, d):
        return sel[d, s]

    def transpose(i, carry):
        for u in range(4):
            t = cnt[i * 4 + u].T
            cnt_t[i * 4 + u] = t
            rsum[pl.ds(i * 4 + u, 1), :] = jnp.sum(t.astype(F32), axis=0, keepdims=True)
        return carry

    def ag_step(t, carry):
        h = t % 2

        def take(r):
            ag_wait(r, h)
            ag_partner(shard(r, h), r, h).start()

        @pl.when(t < 2)
        def _():
            up, down = rw(z - 2, k), rw(z + 2, k)
            ag_wait(up, h)
            ag_send(shard(up, h), up, h, 4, 1).start()

            @pl.when(h == 0)
            def _():
                ag_send(shard(up, h), up, h, 6, 2).start()

            ag_wait(down, h)
            ag_send(shard(down, h), down, h, 5, -1).start()

            @pl.when(h == 1)
            def _():
                ag_send(shard(down, h), down, h, 6, -2).start()

            ag_partner(shard(up, h), up, h).start()
            ag_partner(shard(down, h), down, h).start()
            take(rw(z - 1, k))
            take(rw(z + 1, k))

        @pl.when(t == 2)
        def _():
            take(rw(z - 3, k))
            take(rw(z + 3, k))
            take(rw(z + 4, k))

        @pl.when(t < 2)
        def _():
            lax.fori_loop(16 + t * 8, 24 + t * 8, transpose, 0)

        @pl.when(t == 0)
        def _():
            for h in range(2):
                ag_wait(partner, h)

        @pl.when(t == 2)
        def _():
            for h in range(2):
                ag_wait(rw(z - 1, kp), h)
                ag_wait(rw(z + 1, kp), h)

        dz = (t + 1) // 2
        s0 = rw(z - dz, (k + (t // 2) * (3 - t)) % 2)
        s1 = rw(z + dz, (k + (t + 1) % 2) % 2)
        spmm(cnt, fwd_pick, source_rows, (s0, s1))

        @pl.when(t == 3)
        def _():
            take(rw(z - 3, k))
            take(rw(z + 3, k))
            take(rw(z + 4, k))

        return carry

    lax.fori_loop(0, 16, transpose, 0)
    lax.fori_loop(0, 4, ag_step, 0)

    hot = ((line // 8) * 2 + line % 8 == dst_ids[...]) & (line % 8 < 2) & used
    hot = jnp.where(hot, 1.0, 0.0).astype(BF16)
    part_a = jnp.minimum(rsum[...], 256.0)
    part_b = rsum[...] - part_a
    part_deg = jnp.dot(hot, part_a.astype(BF16), preferred_element_type=F32) + jnp.dot(
        hot, part_b.astype(BF16), preferred_element_type=F32
    )
    dg0[...] = part_deg.reshape(NX, NY, 8, 128)

    def send_dx(j):
        return rcopy(dg0.at[xm(j)], dg1.at[x], dgx_s, dgx_r, col=cl(xm(j), y))

    def send_dy(j):
        return rcopy(dg2.at[ym(j)], dg3.at[y], dgy_s, dgy_r, col=cl(x, ym(j)))

    for j in range(1, NX):
        send_dx(j).start()
    dg1[x] = dg0[x]

    for h in range(2):
        for dz in (2, 3):
            ag_wait(rw(z - dz, kp), h)
            ag_wait(rw(z + dz, kp), h)
        ag_wait(rw(z - 4, kp), h)

    def send_a(jx, yy):
        return rcopy(
            sa.at[xm(jx), yy], ra.at[x, yy], sa_s, sa_r.at[x, yy], col=cl(xm(jx), y)
        )

    def send_b(jy, xx):
        return rcopy(
            sb.at[ym(jy), xx], rb.at[y, xx], sb_s, sb_r.at[y, xx], col=cl(x, ym(jy))
        )

    def emit(jx, carry):
        xx = xm(jx)

        def rest(i, carry):
            shards = ()
            for g in (2 * i, 2 * i + 1):
                dz = 2 + (g + 1) // 2
                shards += (
                    rw(z - dz, (k + (g + 1) % 2) % 2),
                    rw(z + dz, (k + (g + 1) % 2 + g // 3) % 2),
                )
            spmm_block(cnt, fwd_pick, source_rows, xx, 8, shards)
            return carry

        lax.fori_loop(0, 2, rest, 0)

        def put(yy, carry):
            r = pl.ds(pl.multiple_of(cl(xx, yy) * 256, 256), 256)
            sa[xx, yy] = acc[r, 0:128].astype(BF16)
            sb[yy, xx] = acc[r, 128:256].astype(BF16)
            return carry

        lax.fori_loop(0, NY, put, 0)

        @pl.when(jx < 4)
        def _():
            for j in range(1, NY + 1):
                send_a(jx, ym(j)).start()

        for j in range(1, NY):
            send_b(j, xx).start()
        return carry

    lax.fori_loop(1, 5, emit, 0)
    lax.fori_loop(0, 16, zero_acc, 0)
    rcopy(dg1.at[0:3], dg1.at[0:3], dgx_s, dgx_r, row=partner).wait_recv()
    dg2[...] = dg1[0] + dg1[1] + dg1[2] + dg1[3]
    for j in range(1, NY):
        send_dy(j).start()

    def send_a2(j):
        return rcopy(s2a.at[ym(j)], r2a.at[y], s2a_s, s2a_r, col=cl(x, ym(j)))

    def send_b2(j):
        return rcopy(s2b.at[xm(j)], r2b.at[x], s2b_s, s2b_r, col=cl(xm(j), y))

    def sum_a(yy):
        return (
            sa[x, yy].astype(F32)
            + ra[xm(1), yy].astype(F32)
            + ra[xm(2), yy].astype(F32)
            + ra[xm(3), yy].astype(F32)
        )

    def sum_b(xx):
        return (
            sb[y, xx].astype(F32)
            + rb[ym(1), xx].astype(F32)
            + rb[ym(2), xx].astype(F32)
            + rb[ym(3), xx].astype(F32)
        )

    def wait_b(xx):
        for j in range(1, NY):
            part = rb.at[ym(j), xx]
            rcopy(part, part, sb_s, sb_r.at[ym(j), xx], col=me_c).wait_recv()

    def stage_b2(j, carry):
        wait_b(xm(j))
        s2b[xm(j)] = sum_b(xm(j)).astype(BF16)
        send_b2(j).start()
        return carry

    lax.fori_loop(1, NX, stage_b2, 0)

    def wait_a(yy):
        for j in range(1, NX):
            part = ra.at[xm(j), yy]
            rcopy(part, part, sa_s, sa_r.at[xm(j), yy], col=me_c).wait_recv()

    def stage_a2(j, carry):
        wait_a(ym(j))
        s2a[ym(j)] = sum_a(ym(j)).astype(BF16)
        send_a2(j).start()
        return carry

    lax.fori_loop(1, NY, stage_a2, 0)
    wait_a(y)
    wait_b(x)
    nsum[:, 0:128] = sum_a(y)
    nsum[:, 128:256] = sum_b(x)

    dg3[y] = dg2[y]
    rcopy(dg3.at[0:3], dg3.at[0:3], dgy_s, dgy_r, row=partner).wait_recv()
    degree = dg3[0] + dg3[1] + dg3[2] + dg3[3]
    inv_lane = 1.0 / jnp.sqrt(degree + 1.0)
    eye = line == lane
    inv_col = jnp.concatenate(
        [
            jnp.sum(jnp.where(eye, inv_lane[b : b + 1, :], 0.0), axis=1, keepdims=True)
            for b in range(2)
        ],
        axis=0,
    )

    rcopy(r2a.at[0:3], r2a.at[0:3], s2a_s, s2a_r, row=partner).wait_recv()
    nsum[:, 0:128] += (
        r2a[ym(1)].astype(F32) + r2a[ym(2)].astype(F32) + r2a[ym(3)].astype(F32)
    )
    rcopy(r2b.at[0:3], r2b.at[0:3], s2b_s, s2b_r, row=partner).wait_recv()
    nsum[:, 128:256] += (
        r2b[xm(1)].astype(F32) + r2b[xm(2)].astype(F32) + r2b[xm(3)].astype(F32)
    )

    for copy in inputs:
        copy.wait()
    agg[...] = (nsum[...] * inv_col).astype(BF16)
    pre = (
        jnp.dot(feat[...], w_self[...], preferred_element_type=F32)
        + jnp.dot(agg[...], w_neigh[...], preferred_element_type=F32)
        + bias[...]
    )
    sig = jax.nn.sigmoid(pre)
    layer_out[...] = (pre * sig).astype(BF16)
    gpre[...] = (cot[...].astype(F32) * sig * (1.0 + pre * (1.0 - sig))).astype(BF16)
    gsum = (
        lax.dot_general(gpre[...], w_neigh[...], nt, preferred_element_type=F32) * inv_col
    ).astype(BF16)
    dtab[me_c, 0] = gsum[:, 0:128]
    dtab[me_c, 1] = gsum[:, 128:256]

    def full_x(j):
        return rcopy(dtab.at[me_c], dtab.at[me_c], df_s, df_r.at[me_c], col=cl(xm(j), y))

    def full_y(j):
        return rcopy(dtab.at[me_c], dtab.at[me_c], df_s, df_r.at[me_c], col=cl(x, ym(j)))

    def half_a(jx, jy):
        part = dtab.at[cl(xm(jx), y), 0]
        return rcopy(
            part, part, da_s, da_r.at[cl(xm(jx), y)], col=cl(x, ym(jy))
        )

    def half_b(jx, jy):
        part = dtab.at[cl(x, ym(jy)), 1]
        return rcopy(
            part, part, db_s, db_r.at[cl(x, ym(jy))], col=cl(xm(jx), y)
        )

    def start_full(j, carry):
        full_x(j).start()
        full_y(j).start()
        return carry

    lax.fori_loop(1, 4, start_full, 0)

    grad_self[...] = lax.dot_general(
        gpre[...], w_self[...], nt, preferred_element_type=F32
    ).astype(BF16)
    gwb[0, 0:256, :] = lax.dot_general(feat[...], gpre[...], tn, preferred_element_type=F32)
    gwb[1, 0:256, :] = lax.dot_general(agg[...], gpre[...], tn, preferred_element_type=F32)
    gb = jnp.broadcast_to(jnp.sum(gpre[...].astype(F32), axis=0, keepdims=True), (8, 256))
    gwb[0, 256:264, :] = gb
    gwb[1, 256:264, :] = gb

    def send_w0():
        return rcopy(gwb.at[kp], gwr, w0_s, w0_r, row=partner)

    def send_w1(j):
        zz = zm(z + j)
        return rcopy(w1s.at[zz], w1r.at[z], w1_s, w1_r, row=rw(zz, k))

    def send_w2(j):
        return rcopy(wz.at[z], wz.at[z], w2_s, w2_r, row=rw(z + j, k))

    def send_x1(j):
        c = (me_c + j) % 16
        return rcopy(x1s.at[c], x1r.at[me_c], x1_s, x1_r, col=c)

    def send_x2(j):
        part = gfin.at[k, me_c]
        return rcopy(part, part, x2_s, x2_r, col=(me_c + j) % 16)

    def send_pf():
        return rcopy(gfin.at[k], gfin.at[k], pf_s, pf_r, row=partner)

    send_w0().start()

    def take_x(jx):
        c = cl(xm(jx), y)
        rcopy(dtab.at[c], dtab.at[c], df_s, df_r.at[c], col=me_c).wait_recv()

        def go(jy, carry):
            half_a(jx, jy).start()
            return carry

        lax.fori_loop(1, 4, go, 0)

    def take_y(jy):
        c = cl(x, ym(jy))
        rcopy(dtab.at[c], dtab.at[c], df_s, df_r.at[c], col=me_c).wait_recv()

        def go(jx, carry):
            half_b(jx, jy).start()
            return carry

        lax.fori_loop(1, 4, go, 0)

    def take_rest(c):
        part = dtab.at[c, 0]
        rcopy(part, part, da_s, da_r.at[c], col=me_c).wait_recv()
        part = dtab.at[c, 1]
        rcopy(part, part, db_s, db_r.at[c], col=me_c).wait_recv()

    send_w0().wait_recv()
    gwb[k] = gwb[k] + gwr[...]

    def split_z(j, carry):
        w1s[j, 0:32, :] = gwb[k, pl.ds(pl.multiple_of(j * 32, 32), 32), :].astype(BF16)
        w1s[j, 32:48, :] = jnp.concatenate([gwb[k, 256:264, :]] * 2, axis=0).astype(BF16)
        return carry

    lax.fori_loop(0, NZ, split_z, 0)
    for j in range(1, NZ):
        send_w1(j).start()
    w1r[z] = w1s[z]
    take_x(1)
    take_y(1)
    take_x(3)
    take_y(3)

    def order(q):
        m = q - 7
        dx = jnp.where(q < 4, q, jnp.where(q < 7, 0, 1 + m // 3))
        dy = jnp.where(q < 4, 0, jnp.where(q < 7, q - 3, 1 + m % 3))
        return cl(xm(dx), ym(dy))

    def bwd_step(g, carry):
        @pl.when(g == 1)
        def _():
            take_x(2)
            take_y(2)

        @pl.when(g == 3)
        def _():
            rcopy(w1r.at[0:7], w1r.at[0:7], w1_s, w1_r, row=partner).wait_recv()
            tot = w1r[0].astype(F32)
            for j in range(1, NZ):
                tot = tot + w1r[j].astype(F32)
            wz[z] = tot[0:32]
            gwb[k, 256:264, :] = tot[32:40]
            for j in range(1, NZ):
                send_w2(j).start()

        @pl.when(g > 3)
        def _():
            take_rest(order(2 * g))

        @pl.when(g > 2)
        def _():
            take_rest(order(2 * g + 1))

        spmm(cnt_t, bwd_pick, grad_rows, (order(2 * g), order(2 * g + 1)))
        return carry

    lax.fori_loop(0, 6, bwd_step, 0)
    last = tuple(order(q) for q in range(12, 16))
    for c in last:
        take_rest(c)

    def chunk(zz, kk):
        return acc[pl.ds(pl.multiple_of(rw(zz, kk) * 256, 256), 256), :]

    def send_p(zz):
        return rcopy(psend.at[zz], precv.at[zz], p_s, p_r.at[zz], row=partner)

    def put_p(zz):
        psend[zz] = chunk(zz, kp).astype(BF16)
        send_p(zz).start()

    def finish(zz):
        spmm_block(cnt_t, bwd_pick, grad_rows, zz, 4, last)
        put_p(zz)

    def rows_of(h):
        return pl.ds(pl.multiple_of(h * 128, 128), 128)

    def own_part(zz, h):
        r = pl.ds(pl.multiple_of(rw(zz, k) * 256 + h * 128, 128), 128)
        return acc[r, :] + precv[zz, rows_of(h), :].astype(F32)

    def send_e3(i, h):
        return rcopy(
            esend.at[i, h], e3.at[i, h], e_s, e3_r.at[i, h], row=rw(z + 1 - 2 * i, k)
        )

    def send_e4(i):
        return rcopy(esend.at[2, i], e4.at[i], e_s, e4_r.at[i], row=rw(z + 2 - 4 * i, k))

    def send_f1(i, h):
        return rcopy(
            esend.at[3 + i, h], f1.at[i, h], e_s, f1_r.at[i, h], row=rw(z + 1 - 2 * i, k)
        )

    def send_f2(i, h):
        return rcopy(
            esend.at[5 + i, h], f2.at[i, h], e_s, f2_r.at[i, h], row=rw(z + 2 - 4 * i, k)
        )

    def finish_at(j, carry):
        dz = (3 + 2 * j) * (j < 2) + 4 * (j == 2) + (2 + 4 * (j - 3)) * ((j > 2) & (j < 5)) + (
            1 + 6 * (j - 5)
        ) * ((j > 4) & (j < 7))
        finish(zm(z + dz))
        return carry

    lax.fori_loop(0, 3, finish_at, 0)

    def first_hop(i, carry):
        zz = zm(z + 3 + 2 * i)
        send_p(zz).wait_recv()
        for h in range(2):
            esend[i, h] = own_part(zz, h).astype(BF16)
            send_e3(i, h).start()
        return carry

    lax.fori_loop(0, 2, first_hop, 0)
    send_p(zm(z + 4)).wait_recv()
    for h in range(2):
        esend[2, h] = own_part(zm(z + 4), h).astype(BF16)
        send_e4(h).start()

    lax.fori_loop(3, 8, finish_at, 0)

    def to_next(i, carry):
        zz = zm(z + 1 + 6 * i)
        send_p(zz).wait_recv()
        for h in range(2):
            esend[3 + i, h] = own_part(zz, h).astype(BF16)
            send_f1(i, h).start()
        return carry

    lax.fori_loop(0, 2, to_next, 0)

    def to_second(i, carry):
        zz = zm(z + 2 + 4 * i)
        send_p(zz).wait_recv()
        for h in range(2):
            send_e3(i, h).wait_recv()

            @pl.when(i == h)
            def _():
                send_e4(h).wait_recv()
                esend[5 + i, h] = (
                    own_part(zz, h) + e3[i, h].astype(F32) + e4[h].astype(F32)
                ).astype(BF16)

            @pl.when(i != h)
            def _():
                esend[5 + i, h] = (own_part(zz, h) + e3[i, h].astype(F32)).astype(BF16)

            send_f2(i, h).start()
        return carry

    lax.fori_loop(0, 2, to_second, 0)

    rcopy(wz.at[0:7], wz.at[0:7], w2_s, w2_r, row=partner).wait_recv()

    def split_c(i, carry):
        for u in range(2):
            x1s[2 * i + u, 0:16, :] = wz[i, u * 16 : u * 16 + 16, :]
            x1s[2 * i + u, 16:24, :] = gwb[k, 256:264, :]
        return carry

    lax.fori_loop(0, NZ, split_c, 0)
    x1r[me_c] = x1s[me_c]

    def start_x1(j, carry):
        send_x1(j).start()
        return carry

    lax.fori_loop(1, NX * NY, start_x1, 0)

    rcopy(x1r.at[0:15], x1r.at[0:15], x1_s, x1_r, row=partner).wait_recv()
    tot = x1r[0]
    for c in range(1, NX * NY):
        tot = tot + x1r[c]
    g_b[...] = tot[16:17] * scale
    gfin[k, me_c] = tot[0:16] * scale

    def start_x2(j, carry):
        send_x2(j).start()
        return carry

    lax.fori_loop(1, NX * NY, start_x2, 0)
    send_p(z).wait_recv()
    for h in range(2):
        for i in range(2):
            send_f1(i, h).wait_recv()
        nsum[h * 128 : h * 128 + 128, :] = (
            own_part(z, h) + f1[0, h].astype(F32) + f1[1, h].astype(F32)
        )

    rcopy(gfin.at[k, 0:15], gfin.at[k, 0:15], x2_s, x2_r, row=partner).wait_recv()
    send_pf().start()
    for h in range(2):
        for i in range(2):
            send_f2(i, h).wait_recv()
        grad_source[h * 128 : h * 128 + 128, :] = (
            nsum[h * 128 : h * 128 + 128, :] + f2[0, h].astype(F32) + f2[1, h].astype(F32)
        ).astype(BF16)
    rcopy(gfin.at[kp], gfin.at[kp], pf_s, pf_r, row=partner).wait_recv()
    g_ws[...] = gfin[0].reshape(256, 256)
    g_wn[...] = gfin[1].reshape(256, 256)

    def sent(buf, sem):
        rcopy(buf, buf, sem, ag_r.at[0, 0], row=partner).wait_send()

    sent(tab.at[0:7], ag_s)
    sent(tab.at[0:8], ag_sp)
    sent(sa.at[0:3], sa_s)
    sent(sb.at[0:3], sb_s)
    sent(s2a.at[0:3], s2a_s)
    sent(s2b.at[0:3], s2b_s)
    sent(dg0.at[0:3], dgx_s)
    sent(dg2.at[0:3], dgy_s)
    sent(dtab.at[0:6], df_s)
    sent(dtab.at[0:9, 0], da_s)
    sent(dtab.at[0:9, 1], db_s)
    sent(w1s.at[0:7], w1_s)
    sent(wz.at[0:7], w2_s)
    sent(x1s.at[0:15], x1_s)
    sent(gfin.at[k, 0:15], x2_s)
    sent(psend, p_s)
    sent(esend, e_s)
    send_w0().wait_send()
    send_pf().wait_send()


def hand_over(*refs):
    n = len(refs) // 2
    for i in range(n):
        refs[n + i][...] = refs[i][...]


def body(
    source_emb, self_feat, w_self, w_neigh, bias, cotangent, tile_dst, tile_src, tile_live, tile_counts
):
    counts = tile_counts.reshape(SLOTS, 128, 128)
    dst, src = tile_dst.reshape(1, SLOTS), tile_src.reshape(1, SLOTS)
    scale = 1.0 / math.sqrt(self_feat.shape[0] * lax.axis_size("row") * lax.axis_size("col"))
    vm = pl.BlockSpec(memory_space=pltpu.VMEM)
    dma = pltpu.SemaphoreType.DMA
    v = pltpu.VMEM
    outs = pl.pallas_call(
        functools.partial(kernel, scale),
        out_shape=(
            jax.ShapeDtypeStruct((256, 256), BF16),
            jax.ShapeDtypeStruct((256, 256), BF16),
            jax.ShapeDtypeStruct((256, 256), BF16),
            jax.ShapeDtypeStruct((256, 256), F32),
            jax.ShapeDtypeStruct((256, 256), F32),
            jax.ShapeDtypeStruct((1, 256), F32),
        ),
        in_specs=[pl.BlockSpec(memory_space=pltpu.SMEM)] * 3 + [vm] * 3 + [pl.BlockSpec(memory_space=pl.ANY)] * 6,
        out_specs=(vm,) * 6,
        scratch_shapes=[
            v((256, 256), BF16),
            v((256, 256), BF16),
            v((256, 256), BF16),
            v((1, 256), F32),
            v((256, 256), BF16),
            pltpu.SMEM((NB, 128), jnp.int32),
            v((NB, 128), jnp.int32),
            v((SLOTS, 128, 128), jnp.int32),
            v((SLOTS + 1, 128, 128), BF16),
            v((SLOTS + 1, 128, 128), BF16),
            v((4096, 256), F32),
            v((16, 2, 128, 256), BF16),
            v((NX, NY, 256, 128), BF16),
            v((NY, NX, 256, 128), BF16),
            v((NX, NY, 256, 128), BF16),
            v((NY, NX, 256, 128), BF16),
            v((NY, 256, 128), BF16),
            v((NX, 256, 128), BF16),
            v((NY, 256, 128), BF16),
            v((NX, 256, 128), BF16),
            v((256, 256), F32),
            v((SLOTS, 128), F32),
            v((NX, NY, 8, 128), F32),
            v((NX, NY, 8, 128), F32),
            v((NY, 8, 128), F32),
            v((NY, 8, 128), F32),
            v((256, 256), BF16),
            v((256, 256), BF16),
            v((16, 2, 256, 128), BF16),
            v((2, 264, 256), F32),
            v((264, 256), F32),
            v((NZ, 48, 256), BF16),
            v((NZ, 48, 256), BF16),
            v((NZ, 32, 256), F32),
            v((16, 24, 256), F32),
            v((16, 24, 256), F32),
            v((2, 16, 16, 256), F32),
            v((NZ, 256, 256), BF16),
            v((NZ, 256, 256), BF16),
            v((7, 2, 128, 256), BF16),
            v((2, 2, 128, 256), BF16),
            v((2, 128, 256), BF16),
            v((2, 2, 128, 256), BF16),
            v((2, 2, 128, 256), BF16),
            dma((5,)),
            dma((16,)),
            dma,
            dma((16, 2)),
            dma,
            dma,
            dma, dma((4, 4)),
            dma, dma((4, 4)),
            dma, dma,
            dma, dma,
            dma, dma,
            dma, dma,
            dma, dma((16,)),
            dma, dma((16,)),
            dma, dma((16,)),
            dma, dma,
            dma, dma,
            dma, dma,
            dma, dma,
            dma, dma,
            dma, dma,
            dma, dma((NZ,)),
            dma,
            dma((2, 2)),
            dma((2,)),
            dma((2, 2)),
            dma((2, 2)),
        ],
        compiler_params=pltpu.CompilerParams(
            collective_id=0, has_side_effects=True, vmem_limit_bytes=56 * 1024 * 1024
        ),
    )(
        dst, src, tile_live, dst, tile_live,
        source_emb, self_feat, w_self, w_neigh, bias.reshape(1, -1), cotangent, counts,
    )
    outs = pl.pallas_call(
        hand_over,
        out_shape=tuple(jax.ShapeDtypeStruct(o.shape, o.dtype) for o in outs),
        in_specs=[vm] * 6,
        out_specs=(vm,) * 6,
    )(*outs)
    layer_out, grad_self, grad_source, g_ws, g_wn, g_b = outs
    return layer_out, grad_self, grad_source, g_ws, g_wn, g_b.reshape(-1)


def solution(mesh):
    in_specs = (
        P(("col", "row"), None),
        P(("row", "col"), None),
        P(),
        P(),
        P(),
        P(("row", "col"), None),
        P("row", "col", None),
        P("row", "col", None),
        P("row", "col"),
        P("row", "col", None, None, None),
    )
    out_specs = (
        P(("row", "col"), None),
        P(("row", "col"), None),
        P(("col", "row"), None),
        P(),
        P(),
        P(),
    )
    return jax.shard_map(body, mesh=mesh, in_specs=in_specs, out_specs=out_specs, check_vma=False)
```
